256 devices in a mesh: row: 16 (over z_lo, x, core), col: 16 (over y, z_hi).
Axes of the slice: x: 4, y: 4, z: 8 (z_hi: 4, z_lo: 2; z = z_hi * 2 + z_lo), core: 2. Of those that a mesh axis runs over, the one named last changes fastest.
Arguments:
- pair: bfloat16 [768, 768, 128], P('row', 'col'), may hold values from -6 to 6
- ln_gain: float32 [128], replicated, may hold values from 0.25 to 1.75
- w_query: bfloat16 [128, 128], replicated, may hold values from -46 to 46
- w_key: bfloat16 [128, 128], replicated, may hold values from -0.5 to 0.5
- w_value: bfloat16 [128, 128], replicated, may hold values from -0.5 to 0.5
- w_gate: bfloat16 [128, 128], replicated, may hold values from -0.5 to 0.5
- w_bias: bfloat16 [128, 4], replicated, may hold values from -0.5 to 0.5
- w_out: bfloat16 [128, 128], replicated, may hold values from -0.5 to 0.5
- valid_length: int32 [1], replicated, may hold values from 384 to 768
Outputs:
- update: bfloat16 [768, 768, 128], P('row', 'col')
The draws below stay inside these ranges and needn't reach their ends.
Inputs may be any that keep to these rules, and one draw needn't show every extreme that they name: Tokens 0 to valid_length - 1 are real, the others are padding.
All inputs are finite; a program needn't handle non-finite values.
Results may differ from the reference program's by a relative error of at most 0.014.
The reference program's roundings to bfloat16 on the way count: a program that leaves them out, or rounds other values in their place, can miss the bound.
Values may be sent and summed in bfloat16 or wider, within the bound.
No kernel may reach another device: no remote copies, remote signals or barrier semaphores. Data moves between devices by JAX's collectives and lax.ppermute only.
A program may use at most 128 MiB of HBM per device.

```python
import math
import jax
import jax.numpy as jnp
from jax import lax

C = 128
H = 4
DH = 32
N = 768


def draw_w_query(key, part):
    sample = jnp.clip(jax.random.normal(key, (C, H * DH), jnp.float32), -4.0, 4.0) / math.sqrt(C)
    return sample.astype(jnp.bfloat16)


def steps_of(rng, shape, cuts, low, high):
    gain, own = 1.0, jax.random.fold_in(rng, 6)
    for dim, parts in cuts:
        heights = jnp.exp(jax.random.uniform(jax.random.fold_in(own, dim), (parts,), jnp.float32, low / len(cuts), high / len(cuts)))
        gain = gain * jnp.repeat(heights, shape[dim] // parts).reshape([-1 if axis == dim else 1 for axis in range(len(shape))])
    return gain


def normal_values(stream_key, dims, deviation, limit, cuts=(), kind=jnp.bfloat16):
    result = jax.random.normal(stream_key, dims, jnp.float32) * deviation
    if len(cuts) > 0:
        result = steps_of(stream_key, dims, cuts, -0.22, 0.18) * result
    return jnp.clip(result, min=-limit, max=limit).astype(kind)


def setup_inputs(seed: int = 0) -> dict:
    arg_keys = jax.random.split(jax.random.key(seed), 10)
    return {
        "pair": normal_values(arg_keys[0], (N, N, C), 1.0, 6.0, ((0, 16), (1, 16))),
        "ln_gain": jnp.clip(1.0 + 0.15 * jax.random.normal(arg_keys[1], (C,), jnp.float32), 0.25, 1.75),
        "w_query": draw_w_query(jax.random.fold_in(arg_keys[9], 71), 0),
        "w_key": normal_values(arg_keys[3], (C, H * DH), C ** -0.5, 0.5),
        "w_value": normal_values(arg_keys[4], (C, H * DH), C ** -0.5, 0.5),
        "w_gate": normal_values(arg_keys[5], (C, H * DH), C ** -0.5, 0.5),
        "w_bias": normal_values(arg_keys[6], (C, H), C ** -0.5, 0.5),
        "w_out": normal_values(arg_keys[7], (H * DH, C), (H * DH) ** -0.5, 0.5),
        "valid_length": jax.random.randint(arg_keys[8], (1,), N // 2, N + 1).astype(jnp.int32),
    }


epsilon = 1e-05

def normalize(pair_rows, ln_gain):
    widened = pair_rows.astype(jnp.float32)
    average = lax.optimization_barrier(jnp.mean(widened, -1, keepdims=True))
    centred = widened - average
    spread = lax.optimization_barrier(jnp.mean(centred * centred, -1, keepdims=True))
    return (centred * lax.rsqrt(spread + epsilon) * ln_gain).astype(jnp.bfloat16)

def reference(pair, ln_gain, w_query, w_key, w_value, w_gate, w_bias, w_out, valid_length):
    length = valid_length[0]
    query_scale = DH ** (-0.5)
    positions = jnp.arange(N, dtype=jnp.int32)
    key_valid = positions < length

    def bias_row(pair_row):
        normed = normalize(pair_row, ln_gain)
        return jnp.dot(normed, w_bias, preferred_element_type=jnp.float32).astype(jnp.bfloat16)
    bias_all = lax.map(bias_row, pair)
    bias_heads = jnp.transpose(bias_all, (2, 0, 1)).astype(jnp.float32)

    def attend_row(inputs):
        pair_row, row_index = inputs
        normed = normalize(pair_row, ln_gain)
        query = (jnp.dot(normed, w_query, preferred_element_type=jnp.float32) * query_scale).astype(jnp.bfloat16)
        key_proj = jnp.dot(normed, w_key, preferred_element_type=jnp.float32).astype(jnp.bfloat16)
        value_proj = jnp.dot(normed, w_value, preferred_element_type=jnp.float32).astype(jnp.bfloat16)
        gating = jax.nn.sigmoid(jnp.dot(normed, w_gate, preferred_element_type=jnp.float32)).astype(jnp.bfloat16)
        query_heads = query.reshape(N, H, DH).astype(jnp.float32)
        key_heads = key_proj.reshape(N, H, DH).astype(jnp.float32)
        value_heads = value_proj.reshape(N, H, DH).astype(jnp.float32)
        scores = jnp.einsum('jhd,khd->hjk', query_heads, key_heads) + bias_heads
        scores = jnp.where(key_valid[None, None, :], scores, -1e+30)
        highest = lax.optimization_barrier(jnp.max(scores, -1, keepdims=True))
        exponent = jnp.exp(scores - highest)
        totals = lax.optimization_barrier(jnp.sum(exponent, -1))
        weights = exponent.astype(jnp.bfloat16).astype(jnp.float32)
        blended = jnp.einsum('hjk,khd->jhd', weights, value_heads) / jnp.transpose(totals)[:, :, None]
        gated = (gating.astype(jnp.float32) * blended.reshape(N, H * DH)).astype(jnp.bfloat16)
        update = jnp.dot(gated, w_out, preferred_element_type=jnp.float32)
        inside = (row_index < length) & key_valid
        return jnp.where(inside[:, None], update, 0.0).astype(jnp.bfloat16)
    return lax.map(attend_row, (pair, positions))
```

```python
import functools
import jax
import jax.numpy as jnp
from jax import lax
from jax.experimental import pallas as pl
from jax.experimental.pallas import tpu as pltpu
from jax.sharding import Mesh, PartitionSpec as P

epsilon = 1e-05
bf16, f32 = jnp.bfloat16, jnp.float32


def contract(a, b, da, db):
    return lax.dot_general(a, b, (((da,), (db,)), ((), ())), preferred_element_type=f32)


def prepare(pair_ref, gain_ref, wide_ref, normed_ref, bias_ref, *, step):
    rows, cols, channels = pair_ref.shape
    half = cols // 2
    lanes = wide_ref.shape[1]
    gain = gain_ref[...]
    lane = lax.broadcasted_iota(jnp.int32, (half, lanes), 1)
    first = lane < lanes // 2
    lane_j = lax.rem(lane, rows)

    def chunk(g, acc):
        start = g * step
        x = pair_ref[pl.ds(start, step)].reshape(step * cols, channels).astype(f32)
        centred = x - jnp.mean(x, -1, keepdims=True)
        spread = jnp.mean(centred * centred, -1, keepdims=True)
        normed = (centred * lax.rsqrt(spread + epsilon) * gain).astype(bf16)
        normed_ref[pl.ds(start, step)] = normed.reshape(step, cols, channels)
        wide = contract(normed, wide_ref[...], 1, 0)
        for t in range(step):
            one = wide[t * cols : (t + 1) * cols]
            both = jnp.where(first, one[:half], one[half:])
            acc = jnp.where(lane_j == start + t, both, acc)
        return acc

    bias = lax.fori_loop(0, rows // step, chunk, jnp.zeros((half, lanes), f32)).astype(bf16)
    for c in range(bias_ref.shape[0]):
        bias_ref[c] = bias


def attend(scalars, own_ref, other_ref, bias_ref, wq_ref, wk_ref, wv_ref, wg_ref, wo_ref, out_ref,
           table, rows_buf, key_buf, value_buf, gated_buf, *, heads, scale):
    length, core = scalars[0], scalars[1]
    blocks, each, width, channels = own_ref.shape
    slots = bias_ref.shape[0]
    half = width // 2
    head = channels // heads
    keys, queries = blocks * width, slots * width

    def build(c, carry):
        pieces = [bias_ref[q, c].astype(f32) for q in range(slots)]
        for kh in range(2):
            start = pl.multiple_of(c * width + kh * half, 8)
            pos = start + lax.broadcasted_iota(jnp.int32, (half, queries), 0)
            for h in range(heads):
                lo = (kh * heads + h) * width
                joined = jnp.concatenate([p[:, lo : lo + width] for p in pieces], axis=1)
                table[h, pl.ds(start, half), :] = jnp.where(pos < length, joined, -1e30)
        return carry

    lax.fori_loop(0, blocks, build, 0)
    lane = lax.broadcasted_iota(jnp.int32, (queries, channels), 1)

    def one_row(n, carry):
        side, t = n // each, lax.rem(n, each)

        @pl.when(side == 0)
        def _():
            for c in range(blocks):
                rows_buf[c * width : (c + 1) * width] = own_ref[c, t]

        @pl.when(side == 1)
        def _():
            for c in range(blocks):
                rows_buf[c * width : (c + 1) * width] = other_ref[c, t]

        rows = rows_buf[...]
        key_buf[...] = contract(rows, wk_ref[...], 1, 0).astype(bf16)
        value_buf[...] = contract(wv_ref[...], rows, 1, 1).astype(bf16)
        asked = jnp.concatenate(
            [rows_buf[pl.ds(pl.multiple_of((2 * q + core) * width, 16), width)] for q in range(slots)], axis=0
        )
        query = (contract(asked, wq_ref[...], 1, 0) * scale).astype(bf16)
        gating = jax.nn.sigmoid(contract(wg_ref[...], asked, 1, 1)).astype(bf16).astype(f32)
        for h in range(heads):
            mine = jnp.where((lane >= h * head) & (lane < (h + 1) * head), query, jnp.zeros_like(query))
            scores = contract(key_buf[...], mine, 1, 1) + table[h]
            highest = jnp.max(scores, 0, keepdims=True)
            exponent = jnp.exp(scores - highest)
            totals = jnp.sum(exponent, 0, keepdims=True)
            blended = contract(value_buf[h * head : (h + 1) * head], exponent.astype(bf16), 1, 0)
            blended = blended / totals
            gated_buf[h * head : (h + 1) * head] = (gating[h * head : (h + 1) * head] * blended).astype(bf16)
        update = contract(gated_buf[...], wo_ref[...], 0, 0)
        row_base = jnp.where(side == 0, scalars[2], scalars[3])
        row_ok = row_base + t < length
        place = lax.broadcasted_iota(jnp.int32, (width, channels), 0)
        for q in range(slots):
            ok = (place + (2 * q + core) * width < length) & row_ok
            piece = update[q * width : (q + 1) * width]
            out_ref[side, q, t] = jnp.where(ok, piece, 0.0).astype(bf16)
        return carry

    lax.fori_loop(0, 2 * each, one_row, 0)


ROW, COL, SLOT = ("z_lo", "x", "core"), ("y", "z_hi"), ("z_lo", "x")
VMEM = pl.BlockSpec(memory_space=pltpu.VMEM)
SMEM = pl.BlockSpec(memory_space=pltpu.SMEM)


def run_prepare(pair, ln_gain, w_bias, across):
    tile_rows, tile_cols, channels = pair.shape
    heads = w_bias.shape[1]
    half = tile_cols // 2
    lanes = 2 * heads * tile_rows
    wide = jnp.tile(jnp.repeat(w_bias, tile_rows, axis=1), (1, 2))
    return pl.pallas_call(
        functools.partial(prepare, step=4),
        out_shape=(
            jax.ShapeDtypeStruct(pair.shape, bf16),
            jax.ShapeDtypeStruct((across, half, lanes), bf16),
        ),
        in_specs=[VMEM] * 3,
        out_specs=(VMEM, VMEM),
        name="prepare",
    )(pair, ln_gain.reshape(1, channels), wide)


def run_attend(scalars, own, other, bias, wq, wk, wv, wg, wo, heads):
    blocks, each, width, channels = own.shape
    slots = bias.shape[0]
    keys, queries = blocks * width, slots * width
    head = channels // heads
    return pl.pallas_call(
        functools.partial(attend, heads=heads, scale=head**-0.5),
        out_shape=jax.ShapeDtypeStruct((2, slots, each, width, channels), bf16),
        in_specs=[SMEM] + [VMEM] * 8,
        out_specs=VMEM,
        scratch_shapes=[
            pltpu.VMEM((heads, keys, queries), f32),
            pltpu.VMEM((keys, channels), bf16),
            pltpu.VMEM((keys, channels), bf16),
            pltpu.VMEM((channels, keys), bf16),
            pltpu.VMEM((channels, queries), bf16),
        ],
        compiler_params=pltpu.CompilerParams(vmem_limit_bytes=48 << 20),
        cost_estimate=pl.CostEstimate(flops=2_500_000_000, transcendentals=7_000_000, bytes_accessed=4_000_000),
        name="attend",
    )(scalars, own, other, bias, wq, wk, wv, wg, wo)


def everyone(value, axes, count):
    spread = jnp.broadcast_to(value[None], (count, *value.shape))
    return lax.all_to_all(spread, axes, 0, 0, tiled=True)


def per_device(pair, ln_gain, w_query, w_key, w_value, w_gate, w_bias, w_out, valid_length):
    tile_rows, tile_cols, channels = pair.shape
    heads = w_bias.shape[1]
    across = lax.axis_size(COL)
    slots = lax.axis_size(SLOT)
    each = tile_rows // across
    swap = [(0, 1), (1, 0)]
    normed, bias = run_prepare(pair, ln_gain, w_bias, across)
    bias = lax.all_to_all(bias, COL, 0, 0, tiled=True)
    bias = everyone(bias, SLOT, slots)
    own = lax.all_to_all(normed.reshape(across, each, tile_cols, channels), COL, 0, 0, tiled=True)
    other = lax.ppermute(own, "core", swap)
    core = lax.axis_index("core")
    slot = lax.axis_index(SLOT)
    base = lax.axis_index(COL) * each
    own_base = (2 * slot + core) * tile_rows + base
    other_base = (2 * slot + 1 - core) * tile_rows + base
    scalars = jnp.stack([valid_length[0], core, own_base, other_base]).astype(jnp.int32)
    out = run_attend(scalars, own, other, bias, w_query, w_key, w_value.T, w_gate.T, w_out, heads)
    theirs = lax.ppermute(out[1], "core", swap)
    mine = out[0]
    even = jnp.where(core == 0, mine, theirs)
    odd = jnp.where(core == 0, theirs, mine)
    update = jnp.stack([even, odd], axis=1).reshape(across, each, tile_cols, channels)
    update = lax.all_to_all(update, COL, 0, 0, tiled=True)
    return update.reshape(tile_rows, tile_cols, channels)


def solution(mesh):
    fine = Mesh(mesh.devices.reshape(2, 4, 2, 4, 4), ROW + COL)
    placed = (P(ROW, COL, None), P(), P(), P(), P(), P(), P(), P(), P())
    return jax.shard_map(
        per_device, mesh=fine, in_specs=placed, out_specs=P(ROW, COL, None), check_vma=False
    )
```

```python
import functools
import jax
import jax.numpy as jnp
from jax import lax
from jax.experimental import pallas as pl
from jax.experimental.pallas import tpu as pltpu
from jax.sharding import Mesh, PartitionSpec as P

epsilon = 1e-05
bf16, f32 = jnp.bfloat16, jnp.float32


def contract(a, b, da, db):
    return lax.dot_general(a, b, (((da,), (db,)), ((), ())), preferred_element_type=f32)


def prepare(pair_ref, gain_ref, w_ref, normed_ref, bias_ref, wide_ref, *, step):
    rows, cols, channels = pair_ref.shape
    heads = w_ref.shape[1]
    half = cols // 2
    lanes = wide_ref.shape[1]
    gain = gain_ref[...]
    of_head = lax.rem(lax.broadcasted_iota(jnp.int32, (channels, lanes), 1) // rows, heads)
    weight = w_ref[...].astype(f32)
    wide = jnp.zeros((channels, lanes), f32)
    for h in range(heads):
        wide = jnp.where(of_head == h, weight[:, h : h + 1], wide)
    wide_ref[...] = wide.astype(bf16)
    lane = lax.broadcasted_iota(jnp.int32, (half, lanes), 1)
    first = lane < lanes // 2
    lane_j = lax.rem(lane, rows)

    def chunk(g, acc):
        start = g * step
        x = pair_ref[pl.ds(start, step)].reshape(step * cols, channels).astype(f32)
        centred = x - jnp.mean(x, -1, keepdims=True)
        spread = jnp.mean(centred * centred, -1, keepdims=True)
        normed = (centred * lax.rsqrt(spread + epsilon) * gain).astype(bf16)
        normed_ref[pl.ds(start, step)] = normed.reshape(step, cols, channels)
        wide = contract(normed, wide_ref[...], 1, 0)
        for t in range(step):
            one = wide[t * cols : (t + 1) * cols]
            both = jnp.where(first, one[:half], one[half:])
            acc = jnp.where(lane_j == start + t, both, acc)
        return acc

    bias = lax.fori_loop(0, rows // step, chunk, jnp.zeros((half, lanes), f32)).astype(bf16)
    for c in range(bias_ref.shape[0]):
        bias_ref[c] = bias


def gate(*refs):
    refs[-1][...] = jnp.zeros_like(refs[-1])


def attend(length_ref, own_ref, other_ref, *refs, heads, scale, slots):
    parts_hbm, weights_hbm, refs = refs[:slots], refs[slots : slots + 5], refs[slots + 6 :]
    out_ref, weights, sems, parts, part_sems, table, rows_buf, key_buf, value_buf, gated_buf = refs
    fetches = [pltpu.make_async_copy(p, parts.at[n], part_sems.at[n]) for n, p in enumerate(parts_hbm)]
    copies = [pltpu.make_async_copy(w, weights.at[n], sems.at[n]) for n, w in enumerate(weights_hbm)]
    for copy in fetches + copies:
        copy.start()
    length = length_ref[0]
    blocks, each, width, channels = own_ref.shape
    head = channels // heads
    queries = slots * width
    core, x, z = lax.axis_index("core"), lax.axis_index("x"), lax.axis_index("z_lo")
    along = lax.axis_size("x")
    places = [zz * along + lax.rem(x + by, along) for zz, by in order_of_slots(z, along)]
    block_of = [2 * p + core for p in places]
    base = (lax.axis_index("y") * lax.axis_size("z_hi") + lax.axis_index("z_hi")) * each
    own_base = (2 * (z * along + x) + core) * (each * blocks) + base
    other_base = (2 * (z * along + x) + 1 - core) * (each * blocks) + base
    half = width // 2
    for copy in fetches:
        copy.wait()

    def build(c, carry):
        pieces = [parts[n, c].astype(f32) for n in range(slots)]
        for kh in range(2):
            start = pl.multiple_of(c * width + kh * half, 8)
            pos = start + lax.broadcasted_iota(jnp.int32, (half, queries), 0)
            for h in range(heads):
                lo = (kh * heads + h) * width
                joined = jnp.concatenate([p[:, lo : lo + width] for p in pieces], axis=1)
                table[h, pl.ds(start, half), :] = jnp.where(pos < length, joined, -1e30)
        return carry

    lax.fori_loop(0, blocks, build, 0)
    for copy in copies:
        copy.wait()
    wq, wk, wo = weights[0], weights[1], weights[4]
    wv = weights[2].T
    wg = weights[3].T
    lane = lax.broadcasted_iota(jnp.int32, (queries, channels), 1)

    def one_row(n, carry):
        side, t = n // each, lax.rem(n, each)

        @pl.when(side == 0)
        def _():
            for c in range(blocks):
                rows_buf[c * width : (c + 1) * width] = own_ref[c, t]

        @pl.when(side == 1)
        def _():
            for c in range(blocks):
                rows_buf[c * width : (c + 1) * width] = other_ref[c, t]

        rows = rows_buf[...]
        key_buf[...] = contract(rows, wk, 1, 0).astype(bf16)
        value_buf[...] = contract(wv, rows, 1, 1).astype(bf16)
        asked = jnp.concatenate(
            [rows_buf[pl.ds(pl.multiple_of(b * width, 16), width)] for b in block_of], axis=0
        )
        query = (contract(asked, wq, 1, 0) * scale).astype(bf16)
        gating = jax.nn.sigmoid(contract(wg, asked, 1, 1)).astype(bf16).astype(f32)
        for h in range(heads):
            mine = jnp.where((lane >= h * head) & (lane < (h + 1) * head), query, jnp.zeros_like(query))
            scores = contract(key_buf[...], mine, 1, 1) + table[h]
            highest = jnp.max(scores, 0, keepdims=True)
            exponent = jnp.exp(scores - highest)
            totals = jnp.sum(exponent, 0, keepdims=True)
            blended = contract(value_buf[h * head : (h + 1) * head], exponent.astype(bf16), 1, 0)
            blended = blended / totals
            gated_buf[h * head : (h + 1) * head] = (gating[h * head : (h + 1) * head] * blended).astype(bf16)
        update = contract(gated_buf[...], wo, 0, 0)
        row_base = jnp.where(side == 0, own_base, other_base)
        row_ok = row_base + t < length
        place = lax.broadcasted_iota(jnp.int32, (width, channels), 0)
        for s in range(slots):
            ok = (place + block_of[s] * width < length) & row_ok
            piece = update[s * width : (s + 1) * width]
            out_ref[side, places[s], t] = jnp.where(ok, piece, 0.0).astype(bf16)
        return carry

    lax.fori_loop(0, 2 * each, one_row, 0)


ROW, COL = ("z_lo", "x", "core"), ("y", "z_hi")
VMEM = pl.BlockSpec(memory_space=pltpu.VMEM)
HBM = pl.BlockSpec(memory_space=pltpu.HBM)
SMEM = pl.BlockSpec(memory_space=pltpu.SMEM)


def run_prepare(pair, ln_gain, w_bias, across):
    tile_rows, tile_cols, channels = pair.shape
    heads = w_bias.shape[1]
    half = tile_cols // 2
    lanes = 2 * heads * tile_rows
    return pl.pallas_call(
        functools.partial(prepare, step=16),
        out_shape=(
            jax.ShapeDtypeStruct(pair.shape, bf16),
            jax.ShapeDtypeStruct((across, half, lanes), bf16),
        ),
        in_specs=[VMEM] * 3,
        out_specs=(VMEM, VMEM),
        scratch_shapes=[pltpu.VMEM((channels, lanes), bf16)],
        compiler_params=pltpu.CompilerParams(vmem_limit_bytes=12 << 20),
        name="prepare",
    )(pair, ln_gain.reshape(1, channels), w_bias)


def order_of_slots(z, along):
    near = [(z, 0), (z, along - 1), (z, 1), (1 - z, 0)]
    return near + [(z, along - 2), (1 - z, along - 1), (1 - z, 1), (1 - z, 2)]


def run_gate(arrays):
    return pl.pallas_call(
        gate,
        out_shape=jax.ShapeDtypeStruct((8, 128), f32),
        in_specs=[HBM] * len(arrays),
        out_specs=VMEM,
        compiler_params=pltpu.CompilerParams(vmem_limit_bytes=1 << 20),
        name="gate",
    )(*arrays)


def run_attend(length, own, other, parts, weights, passed, heads):
    blocks, each, width, channels = own.shape
    slots = len(parts)
    keys, queries = blocks * width, slots * width
    head = channels // heads
    return pl.pallas_call(
        functools.partial(attend, heads=heads, scale=head**-0.5, slots=slots),
        out_shape=jax.ShapeDtypeStruct((2, slots, each, width, channels), bf16),
        in_specs=[SMEM] + [VMEM] * 2 + [HBM] * (slots + 6),
        out_specs=VMEM,
        scratch_shapes=[
            pltpu.VMEM((5, channels, channels), bf16),
            pltpu.SemaphoreType.DMA((5,)),
            pltpu.VMEM((slots, *parts[0].shape), bf16),
            pltpu.SemaphoreType.DMA((slots,)),
            pltpu.VMEM((heads, keys, queries), f32),
            pltpu.VMEM((keys, channels), bf16),
            pltpu.VMEM((keys, channels), bf16),
            pltpu.VMEM((channels, keys), bf16),
            pltpu.VMEM((channels, queries), bf16),
        ],
        compiler_params=pltpu.CompilerParams(vmem_limit_bytes=32 << 20),
        cost_estimate=pl.CostEstimate(flops=2_500_000_000, transcendentals=7_000_000, bytes_accessed=4_000_000),
        name="attend",
    )(length, own, other, *parts, *weights, passed)


def shifted(value, axis, by):
    n = lax.axis_size(axis)
    return lax.ppermute(value, axis, [(k, (k + by) % n) for k in range(n)])


def per_device_inner(pair, ln_gain, w_query, w_key, w_value, w_gate, w_bias, w_out, valid_length):
    tile_rows, tile_cols, channels = pair.shape
    heads = w_bias.shape[1]
    across = lax.axis_size(COL)
    each = tile_rows // across
    normed, bias = run_prepare(pair, ln_gain, w_bias, across)
    mine = lax.all_to_all(bias, COL, 0, 0, tiled=True)
    own = lax.all_to_all(normed.reshape(across, each, tile_cols, channels), COL, 0, 0, tiled=True)
    below = shifted(mine, "z_lo", 1)
    left = shifted(mine, "x", 1)
    right = shifted(mine, "x", -1)
    below_left = shifted(below, "x", 1)
    below_right = shifted(below, "x", -1)
    far = shifted(left, "x", 1)
    below_far = shifted(below_right, "x", -1)
    passed = run_gate([right, below_left, far, below_far])
    other = shifted(own, "core", 1)
    parts = [mine, left, right, below, far, below_left, below_right, below_far]
    weights = (w_query, w_key, w_value, w_gate, w_out)
    out = run_attend(valid_length, own, other, parts, weights, passed, heads)
    theirs = shifted(out[1], "core", 1)
    core = lax.axis_index("core")
    even = jnp.where(core == 0, out[0], theirs)
    odd = jnp.where(core == 0, theirs, out[0])
    update = jnp.stack([even, odd], axis=1).reshape(across, each, tile_cols, channels)
    update = lax.all_to_all(update, COL, 0, 0, tiled=True)
    return update.reshape(tile_rows, tile_cols, channels)


def solution(mesh):
    fine = Mesh(mesh.devices.reshape(2, 4, 2, 4, 4), ROW + COL)
    placed = (P(ROW, COL, None), P(), P(), P(), P(), P(), P(), P(), P())
    return jax.shard_map(per_device_inner, mesh=fine, in_specs=placed, out_specs=P(ROW, COL, None), check_vma=False)
```

```python
import functools
import jax
import jax.numpy as jnp
from jax import lax
from jax.experimental import pallas as pl
from jax.experimental.pallas import tpu as pltpu
from jax.sharding import Mesh, PartitionSpec as P

epsilon = 1e-05
bf16, f32 = jnp.bfloat16, jnp.float32


def contract(a, b, da, db):
    return lax.dot_general(a, b, (((da,), (db,)), ((), ())), preferred_element_type=f32)


def prepare(pair_hbm, gain_ref, w_ref, normed_ref, bias_ref, pair_ref, sems, wide_ref, *, step):
    rows, cols, channels = pair_ref.shape
    heads = w_ref.shape[0]
    half = cols // 2
    lanes = wide_ref.shape[1]
    fetches = [
        pltpu.make_async_copy(pair_hbm.at[pl.ds(g * step, step)], pair_ref.at[pl.ds(g * step, step)], sems.at[g])
        for g in range(rows // step)
    ]
    for fetch in fetches:
        fetch.start()
    gain = gain_ref[...]
    slots = 2 * heads
    mine = lax.axis_index("z_lo") * lax.axis_size("x") + lax.axis_index("x")

    def segment(count):
        slot = lax.broadcasted_iota(jnp.int32, (count, lanes), 1) // rows
        return lax.rem(slot + slots - mine, slots)

    own_head = lax.rem(segment(heads), heads) == lax.broadcasted_iota(jnp.int32, (heads, lanes), 0)
    wide_ref[...] = contract(w_ref[...], jnp.where(own_head, 1.0, 0.0).astype(bf16), 0, 0).astype(bf16)
    first = segment(half) < heads
    lane_j = lax.rem(lax.broadcasted_iota(jnp.int32, (half, lanes), 1), rows)
    acc = jnp.zeros((half, lanes), f32)
    for g, fetch in enumerate(fetches):
        fetch.wait()
        start = g * step
        x = pair_ref[pl.ds(start, step)].reshape(step * cols, channels).astype(f32)
        centred = x - jnp.mean(x, -1, keepdims=True)
        spread = jnp.mean(centred * centred, -1, keepdims=True)
        normed = (centred * lax.rsqrt(spread + epsilon) * gain).astype(bf16)
        normed_ref[pl.ds(start, step)] = normed.reshape(step, cols, channels)
        wide = contract(normed, wide_ref[...], 1, 0)
        for t in range(step):
            one = wide[t * cols : (t + 1) * cols]
            both = jnp.where(first, one[:half], one[half:])
            acc = jnp.where(lane_j == start + t, both, acc)
    bias = acc.astype(bf16)
    for c in range(bias_ref.shape[0]):
        bias_ref[c] = bias


def gate(*refs):
    refs[-1][...] = jnp.zeros_like(refs[-1])


def attend(length_ref, own_hbm, other_hbm, *refs, heads, scale, slots):
    parts_hbm, weights_hbm, refs = refs[:slots], refs[slots : slots + 5], refs[slots + 6 :]
    out_ref, weights, sems, parts, part_sems, both, both_sems = refs[:7]
    table = refs[7]
    keys_of, values_of, queries_of, gates_of, gated_of, scores_of = [refs[n : n + 2] for n in range(8, 20, 2)]
    _, blocks, each, width, channels = both.shape
    half = width // 2
    head = channels // heads
    keys, queries = blocks * width, slots * width
    core, x, z = lax.axis_index("core"), lax.axis_index("x"), lax.axis_index("z_lo")
    along = lax.axis_size("x")
    places = [zz * along + lax.rem(x + by, along) for zz, by in order_of_slots(z, along)]
    fetches = [pltpu.make_async_copy(p, parts.at[q], part_sems.at[n]) for n, (p, q) in enumerate(zip(parts_hbm, places))]
    later = [pltpu.make_async_copy(w, weights.at[n], sems.at[n]) for n, w in enumerate(weights_hbm)]
    later += [pltpu.make_async_copy(r, both.at[n], both_sems.at[n]) for n, r in enumerate((own_hbm, other_hbm))]
    for copy in fetches + later:
        copy.start()
    length = length_ref[0]
    base = (lax.axis_index("y") * lax.axis_size("z_hi") + lax.axis_index("z_hi")) * each
    own_base = (2 * (z * along + x) + core) * (each * blocks) + base
    other_base = (2 * (z * along + x) + 1 - core) * (each * blocks) + base
    for ref in values_of:
        ref[:, head:] = jnp.ones_like(ref[:, head:])
    for copy in fetches:
        copy.wait()
    place = lax.broadcasted_iota(jnp.int32, (half, 128), 1)

    def build(c, carry):
        pieces = [parts[q, c].astype(f32) for q in range(slots)]
        for kh in range(2):
            start = pl.multiple_of(c * width + kh * half, 8)
            valid = start + lax.broadcasted_iota(jnp.int32, (half, 128), 0) < length
            for h in range(heads):
                columns = []
                for at in range(0, queries, 128):
                    inside = range(at // width, -(-(at + 128) // width))
                    value = None
                    for p in inside:
                        new = pieces[(p - kh * heads - h) % slots][:, at : at + 128]
                        value = new if value is None else jnp.where(place >= p * width - at, new, value)
                    columns.append(value)
                if kh == 1:
                    turned = [pltpu.roll(v, 64, 1) for v in columns]
                    columns = [jnp.where(place < 64, turned[(n + 1) % 3], turned[(n + 2) % 3]) for n in range(3)]
                for n, value in enumerate(columns):
                    table[h, pl.ds(start, half), n * 128 : (n + 1) * 128] = jnp.where(valid, value, -1e30)
        return carry

    lax.fori_loop(0, blocks, build, 0)
    for copy in later:
        copy.wait()
    chunk = keys // 2
    steps = keys // chunk
    wq, wk, wo = weights[0], weights[1], weights[4]
    wv = weights[2].T
    wg = weights[3].T
    lane = lax.broadcasted_iota(jnp.int32, (width, channels), 1)
    of_head = [(lane >= h * head) & (lane < (h + 1) * head) for h in range(heads)]

    def cells(n, chosen):
        side, t = n // each, lax.rem(n, each)
        return jnp.concatenate([both[side, c, t] for c in chosen], axis=0)

    def project_keys(n, to):
        keys_of[to][...] = contract(cells(n, range(blocks)), wk, 1, 0).astype(bf16)

    def project_values(n, to):
        value = contract(wv, cells(n, range(blocks)), 1, 1).astype(bf16)
        for h in range(heads):
            values_of[to][h, :head] = value[h * head : (h + 1) * head]

    def project_queries(n, to):
        asked = cells(n, [2 * q + core for q in range(slots)])
        query = (contract(asked, wq, 1, 0) * scale).astype(bf16)
        for h in range(heads):
            for p in range(slots):
                q = (p - h) % slots
                block = query[q * width : (q + 1) * width]
                queries_of[to][h, p * width : (p + 1) * width] = jnp.where(of_head[h], block, jnp.zeros_like(block))

    def project_gates(n, to):
        asked = cells(n, [2 * q + core for q in range(slots)])
        gates_of[to][...] = jax.nn.sigmoid(contract(wg, asked, 1, 1)).astype(bf16).astype(f32)

    def score(at, h, k, top):
        part = pl.ds(k * chunk, chunk)
        scores = contract(keys_of[at][part], queries_of[at][h], 1, 1) + table[h, part]
        scores_of[h % 2][part] = scores
        best = jnp.max(scores.reshape(chunk // 8, 8, queries), 0)
        return best if top is None else jnp.maximum(top, best)

    def blend(at, h, k, highest, sofar):
        exponent = jnp.exp(scores_of[h % 2][pl.ds(k * chunk, chunk)] - highest).astype(bf16)
        more = contract(values_of[at][h, :, k * chunk : (k + 1) * chunk], exponent, 1, 0)
        return more if sofar is None else sofar + more

    def one_row(n, at, top):
        following = jnp.minimum(n + 1, 2 * each - 1)
        for h in range(heads):
            highest = jnp.max(top, 0, keepdims=True)
            top, total = None, None
            for k in range(steps):
                if h + 1 < heads:
                    top = score(at, h + 1, k, top)
                else:
                    top = score(1 - at, 0, k, top)
                total = blend(at, h, k, highest, total)
                if h == 0 and k == 0:
                    project_keys(following, 1 - at)
                if h == 0 and k == 1:
                    project_queries(following, 1 - at)
                if h == 1 and k == 0:
                    project_values(following, 1 - at)
                if h == 2 and k == 0:
                    project_gates(following, 1 - at)
            blended = total[:head] / total[head : head + 1]
            if h > 0:
                blended = jnp.concatenate([blended[:, h * width :], blended[:, : h * width]], axis=1)
            part = slice(h * head, (h + 1) * head)
            gated_of[at][part] = (gates_of[at][part] * blended).astype(bf16)
        update = contract(gated_of[at][...], wo, 0, 0)
        side, t = n // each, lax.rem(n, each)
        row_ok = jnp.where(side == 0, own_base, other_base) + t < length
        row = lax.broadcasted_iota(jnp.int32, (width, channels), 0)
        for q in range(slots):
            ok = (row + (2 * q + core) * width < length) & row_ok
            piece = update[q * width : (q + 1) * width]
            out_ref[side, q, t] = jnp.where(ok, piece, 0.0).astype(bf16)
        return top

    for first in (project_keys, project_queries, project_values, project_gates):
        first(0, 0)
    top = None
    for k in range(steps):
        top = score(0, 0, k, top)
    lax.fori_loop(0, each, lambda n, top: one_row(2 * n + 1, 1, one_row(2 * n, 0, top)), top)


ROW, COL = ("z_lo", "x", "core"), ("y", "z_hi")
ALL_VMEM = 67043328
VMEM = pl.BlockSpec(memory_space=pltpu.VMEM)
HBM = pl.BlockSpec(memory_space=pltpu.HBM)
SMEM = pl.BlockSpec(memory_space=pltpu.SMEM)


def run_prepare(pair, ln_gain, w_bias, across):
    tile_rows, tile_cols, channels = pair.shape
    heads = w_bias.shape[1]
    half = tile_cols // 2
    lanes = 2 * heads * tile_rows
    step = 12
    return pl.pallas_call(
        functools.partial(prepare, step=step),
        out_shape=(
            jax.ShapeDtypeStruct(pair.shape, bf16),
            jax.ShapeDtypeStruct((across, half, lanes), bf16),
        ),
        in_specs=[HBM, pl.BlockSpec(), pl.BlockSpec()],
        out_specs=(VMEM, VMEM),
        scratch_shapes=[
            pltpu.VMEM(pair.shape, bf16),
            pltpu.SemaphoreType.DMA((tile_rows // step,)),
            pltpu.VMEM((channels, lanes), bf16),
        ],
        compiler_params=pltpu.CompilerParams(vmem_limit_bytes=ALL_VMEM),
        name="prepare",
    )(pair, ln_gain.reshape(1, channels), w_bias.T)


def order_of_slots(z, along):
    near = [(z, 0), (z, along - 1), (z, 1), (1 - z, 0)]
    return near + [(z, along - 2), (1 - z, along - 1), (1 - z, 1), (1 - z, 2)]


def run_gate(arrays):
    return pl.pallas_call(
        gate,
        out_shape=jax.ShapeDtypeStruct((8, 128), f32),
        in_specs=[HBM] * len(arrays),
        out_specs=VMEM,
        compiler_params=pltpu.CompilerParams(vmem_limit_bytes=1 << 20),
        name="gate",
    )(*arrays)


def run_attend(length, own, other, parts, weights, passed, heads):
    blocks, each, width, channels = own.shape
    slots = len(parts)
    keys, queries = blocks * width, slots * width
    head = channels // heads
    return pl.pallas_call(
        functools.partial(attend, heads=heads, scale=head**-0.5, slots=slots),
        out_shape=jax.ShapeDtypeStruct((2, slots, each, width, channels), bf16),
        in_specs=[SMEM] + [HBM] * (slots + 8),
        out_specs=VMEM,
        scratch_shapes=[
            pltpu.VMEM((5, channels, channels), bf16),
            pltpu.SemaphoreType.DMA((5,)),
            pltpu.VMEM((slots, *parts[0].shape), bf16),
            pltpu.SemaphoreType.DMA((slots,)),
            pltpu.VMEM((2, *own.shape), bf16),
            pltpu.SemaphoreType.DMA((2,)),
            pltpu.VMEM((heads, keys, queries), f32),
        ]
        + [pltpu.VMEM((keys, channels), bf16)] * 2
        + [pltpu.VMEM((heads, head + 16, keys), bf16)] * 2
        + [pltpu.VMEM((heads, queries, channels), bf16)] * 2
        + [pltpu.VMEM((channels, queries), f32)] * 2
        + [pltpu.VMEM((channels, queries), bf16)] * 2
        + [pltpu.VMEM((keys, queries), f32)] * 2,
        compiler_params=pltpu.CompilerParams(vmem_limit_bytes=66060288),
        cost_estimate=pl.CostEstimate(flops=2_500_000_000, transcendentals=7_000_000, bytes_accessed=4_000_000),
        name="attend",
    )(length, own, other, *parts, *weights, passed)


def shifted(value, axis, by):
    n = lax.axis_size(axis)
    return lax.ppermute(value, axis, [(k, (k + by) % n) for k in range(n)])


def per_device_inner(pair, ln_gain, w_query, w_key, w_value, w_gate, w_bias, w_out, valid_length):
    tile_rows, tile_cols, channels = pair.shape
    heads = w_bias.shape[1]
    across = lax.axis_size(COL)
    each = tile_rows // across
    weights = (w_query, w_key, w_value, w_gate, w_out)
    normed, bias = run_prepare(pair, ln_gain, w_bias, across)
    mine = lax.all_to_all(bias, COL, 0, 0, tiled=True)
    own = lax.all_to_all(normed.reshape(across, each, tile_cols, channels), COL, 0, 0, tiled=True)
    below = shifted(mine, "z_lo", 1)
    left = shifted(mine, "x", 1)
    right = shifted(mine, "x", -1)
    below_left = shifted(below, "x", 1)
    below_right = shifted(below, "x", -1)
    far = shifted(left, "x", 1)
    below_far = shifted(below_right, "x", -1)
    passed = run_gate([right, below_left, far, below_far])
    other = shifted(own, "core", 1)
    parts = [mine, left, right, below, far, below_left, below_right, below_far]
    out = run_attend(valid_length, own, other, parts, weights, passed, heads)
    theirs = shifted(out[1], "core", 1)
    core = lax.axis_index("core")
    even = jnp.where(core == 0, out[0], theirs)
    odd = jnp.where(core == 0, theirs, out[0])
    update = jnp.stack([even, odd], axis=1).reshape(across, each, tile_cols, channels)
    update = lax.all_to_all(update, COL, 0, 0, tiled=True)
    return update.reshape(tile_rows, tile_cols, channels)


def solution(mesh):
    fine = Mesh(mesh.devices.reshape(2, 4, 2, 4, 4), ROW + COL)
    placed = (P(ROW, COL, None), P(), P(), P(), P(), P(), P(), P(), P())
    return jax.shard_map(per_device_inner, mesh=fine, in_specs=placed, out_specs=P(ROW, COL, None), check_vma=False)
```

```python
import functools
import jax
import jax.numpy as jnp
from jax import lax
from jax.experimental import pallas as pl
from jax.experimental.pallas import tpu as pltpu
from jax.sharding import Mesh, PartitionSpec as P

epsilon = 1e-05
bf16, f32 = jnp.bfloat16, jnp.float32


def contract(a, b, da, db):
    return lax.dot_general(a, b, (((da,), (db,)), ((), ())), preferred_element_type=f32)


def prepare(pair_hbm, gain_ref, w_ref, normed_hbm, bias_hbm, *refs, step):
    pair_ref, sems, normed_ref, normed_sems, bias_ref, bias_sems, wide_ref = refs
    rows, cols, channels = pair_ref.shape
    heads = w_ref.shape[0]
    half = cols // 2
    lanes = wide_ref.shape[1]
    fetches = [
        pltpu.make_async_copy(pair_hbm.at[pl.ds(g * step, step)], pair_ref.at[pl.ds(g * step, step)], sems.at[g])
        for g in range(rows // step)
    ]
    for fetch in fetches:
        fetch.start()
    gain = gain_ref[...]
    slots = 2 * heads
    mine = lax.axis_index("z_lo") * lax.axis_size("x") + lax.axis_index("x")

    def segment(count):
        slot = lax.broadcasted_iota(jnp.int32, (count, lanes), 1) // rows
        return lax.rem(slot + slots - mine, slots)

    own_head = lax.rem(segment(heads), heads) == lax.broadcasted_iota(jnp.int32, (heads, lanes), 0)
    wide_ref[...] = contract(w_ref[...], jnp.where(own_head, 1.0, 0.0).astype(bf16), 0, 0).astype(bf16)
    first = segment(half) < heads
    lane_j = lax.rem(lax.broadcasted_iota(jnp.int32, (half, lanes), 1), rows)
    acc = jnp.zeros((half, lanes), f32)
    stores = []
    for g, fetch in enumerate(fetches):
        fetch.wait()
        start = g * step
        x = pair_ref[pl.ds(start, step)].reshape(step * cols, channels).astype(f32)
        centred = x - jnp.mean(x, -1, keepdims=True)
        spread = jnp.mean(centred * centred, -1, keepdims=True)
        normed = (centred * lax.rsqrt(spread + epsilon) * gain).astype(bf16)
        normed_ref[pl.ds(start, step)] = normed.reshape(step, cols, channels)
        part = pl.ds(start, step)
        stores.append(pltpu.make_async_copy(normed_ref.at[part], normed_hbm.at[part], normed_sems.at[g]))
        stores[-1].start()
        wide = contract(normed, wide_ref[...], 1, 0)
        for t in range(step):
            one = wide[t * cols : (t + 1) * cols]
            both = jnp.where(first, one[:half], one[half:])
            acc = jnp.where(lane_j == start + t, both, acc)
    bias_ref[...] = acc.astype(bf16)
    for c in range(bias_hbm.shape[0]):
        stores.append(pltpu.make_async_copy(bias_ref, bias_hbm.at[c], bias_sems.at[c]))
        stores[-1].start()
    for store in stores:
        store.wait()


def gate(*refs):
    refs[-1][...] = jnp.zeros_like(refs[-1])


def attend(length_ref, own_hbm, other_hbm, *refs, heads, scale, slots):
    parts_hbm, weights_hbm, refs = refs[:slots], refs[slots : slots + 5], refs[slots + 6 :]
    out_ref, weights, sems, parts, part_sems, both, both_sems = refs[:7]
    table = refs[7]
    keys_of, values_of, queries_of, gates_of, gated_of, scores_of = [refs[n : n + 2] for n in range(8, 20, 2)]
    _, blocks, each, width, channels = both.shape
    half = width // 2
    head = channels // heads
    keys, queries = blocks * width, slots * width
    core, x, z = lax.axis_index("core"), lax.axis_index("x"), lax.axis_index("z_lo")
    along = lax.axis_size("x")
    places = [zz * along + lax.rem(x + by, along) for zz, by in order_of_slots(z, along)]
    fetches = [pltpu.make_async_copy(p, parts.at[q], part_sems.at[n]) for n, (p, q) in enumerate(zip(parts_hbm, places))]
    later = [pltpu.make_async_copy(w, weights.at[n], sems.at[n]) for n, w in enumerate(weights_hbm)]
    later += [pltpu.make_async_copy(r, both.at[n], both_sems.at[n]) for n, r in enumerate((own_hbm, other_hbm))]
    for copy in fetches + later:
        copy.start()
    length = length_ref[0]
    base = (lax.axis_index("y") * lax.axis_size("z_hi") + lax.axis_index("z_hi")) * each
    own_base = (2 * (z * along + x) + core) * (each * blocks) + base
    other_base = (2 * (z * along + x) + 1 - core) * (each * blocks) + base
    for ref in values_of:
        ref[:, head:] = jnp.ones_like(ref[:, head:])
    for copy in fetches:
        copy.wait()
    place = lax.broadcasted_iota(jnp.int32, (half, 128), 1)

    def build(c, carry):
        pieces = [parts[q, c].astype(f32) for q in range(slots)]
        for kh in range(2):
            start = pl.multiple_of(c * width + kh * half, 8)
            valid = start + lax.broadcasted_iota(jnp.int32, (half, 128), 0) < length
            for h in range(heads):
                columns = []
                for at in range(0, queries, 128):
                    inside = range(at // width, -(-(at + 128) // width))
                    value = None
                    for p in inside:
                        new = pieces[(p - kh * heads - h) % slots][:, at : at + 128]
                        value = new if value is None else jnp.where(place >= p * width - at, new, value)
                    columns.append(value)
                if kh == 1:
                    turned = [pltpu.roll(v, 64, 1) for v in columns]
                    columns = [jnp.where(place < 64, turned[(n + 1) % 3], turned[(n + 2) % 3]) for n in range(3)]
                for n, value in enumerate(columns):
                    table[h, pl.ds(start, half), n * 128 : (n + 1) * 128] = jnp.where(valid, value, -1e30)
        return carry

    lax.fori_loop(0, blocks, build, 0)
    for copy in later:
        copy.wait()
    chunk = keys // 2
    steps = keys // chunk
    wq, wk, wo = weights[0], weights[1], weights[4]
    wv = weights[2].T
    wg = weights[3].T
    lane = lax.broadcasted_iota(jnp.int32, (width, channels), 1)
    of_head = [(lane >= h * head) & (lane < (h + 1) * head) for h in range(heads)]

    def cells(n, chosen):
        side, t = n // each, lax.rem(n, each)
        return jnp.concatenate([both[side, c, t] for c in chosen], axis=0)

    def project_keys(n, to):
        keys_of[to][...] = contract(cells(n, range(blocks)), wk, 1, 0).astype(bf16)

    def project_values(n, to):
        value = contract(wv, cells(n, range(blocks)), 1, 1).astype(bf16)
        for h in range(heads):
            values_of[to][h, :head] = value[h * head : (h + 1) * head]

    def project_queries(n, to):
        asked = cells(n, [2 * q + core for q in range(slots)])
        query = (contract(asked, wq, 1, 0) * scale).astype(bf16)
        for h in range(heads):
            for p in range(slots):
                q = (p - h) % slots
                block = query[q * width : (q + 1) * width]
                queries_of[to][h, p * width : (p + 1) * width] = jnp.where(of_head[h], block, jnp.zeros_like(block))

    def project_gates(n, to):
        asked = cells(n, [2 * q + core for q in range(slots)])
        gates_of[to][...] = jax.nn.sigmoid(contract(wg, asked, 1, 1)).astype(bf16).astype(f32)

    def score(at, h, k, top):
        part = pl.ds(k * chunk, chunk)
        scores = contract(keys_of[at][part], queries_of[at][h], 1, 1) + table[h, part]
        scores_of[h % 2][part] = scores
        best = jnp.max(scores.reshape(chunk // 8, 8, queries), 0)
        return best if top is None else jnp.maximum(top, best)

    def blend(at, h, k, highest, sofar):
        exponent = jnp.exp(scores_of[h % 2][pl.ds(k * chunk, chunk)] - highest).astype(bf16)
        more = contract(values_of[at][h, :, k * chunk : (k + 1) * chunk], exponent, 1, 0)
        return more if sofar is None else sofar + more

    def one_row(n, at, top):
        following = jnp.minimum(n + 1, 2 * each - 1)
        for h in range(heads):
            highest = jnp.max(top, 0, keepdims=True)
            top, total = None, None
            for k in range(steps):
                if h + 1 < heads:
                    top = score(at, h + 1, k, top)
                else:
                    top = score(1 - at, 0, k, top)
                total = blend(at, h, k, highest, total)
                if h == 0 and k == 0:
                    project_keys(following, 1 - at)
                if h == 0 and k == 1:
                    project_queries(following, 1 - at)
                if h == 1 and k == 0:
                    project_values(following, 1 - at)
                if h == 2 and k == 0:
                    project_gates(following, 1 - at)
            blended = total[:head] / total[head : head + 1]
            if h > 0:
                blended = jnp.concatenate([blended[:, h * width :], blended[:, : h * width]], axis=1)
            part = slice(h * head, (h + 1) * head)
            gated_of[at][part] = (gates_of[at][part] * blended).astype(bf16)
        update = contract(gated_of[at][...], wo, 0, 0)
        side, t = n // each, lax.rem(n, each)
        row_ok = jnp.where(side == 0, own_base, other_base) + t < length
        row = lax.broadcasted_iota(jnp.int32, (width, channels), 0)
        for q in range(slots):
            ok = (row + (2 * q + core) * width < length) & row_ok
            piece = update[q * width : (q + 1) * width]
            out_ref[side, q, t] = jnp.where(ok, piece, 0.0).astype(bf16)
        return top

    for first in (project_keys, project_queries, project_values, project_gates):
        first(0, 0)
    top = None
    for k in range(steps):
        top = score(0, 0, k, top)
    lax.fori_loop(0, each, lambda n, top: one_row(2 * n + 1, 1, one_row(2 * n, 0, top)), top)


ROW, COL = ("z_lo", "x", "core"), ("y", "z_hi")
ALL_VMEM = 67043328
VMEM = pl.BlockSpec(memory_space=pltpu.VMEM)
HBM = pl.BlockSpec(memory_space=pltpu.HBM)
SMEM = pl.BlockSpec(memory_space=pltpu.SMEM)


def run_prepare(pair, ln_gain, w_bias, across):
    tile_rows, tile_cols, channels = pair.shape
    heads = w_bias.shape[1]
    half = tile_cols // 2
    lanes = 2 * heads * tile_rows
    step = 12
    return pl.pallas_call(
        functools.partial(prepare, step=step),
        out_shape=(
            jax.ShapeDtypeStruct(pair.shape, bf16),
            jax.ShapeDtypeStruct((across, half, lanes), bf16),
        ),
        in_specs=[HBM, pl.BlockSpec(), pl.BlockSpec()],
        out_specs=(HBM, HBM),
        scratch_shapes=[
            pltpu.VMEM(pair.shape, bf16),
            pltpu.SemaphoreType.DMA((tile_rows // step,)),
            pltpu.VMEM(pair.shape, bf16),
            pltpu.SemaphoreType.DMA((tile_rows // step,)),
            pltpu.VMEM((half, lanes), bf16),
            pltpu.SemaphoreType.DMA((across,)),
            pltpu.VMEM((channels, lanes), bf16),
        ],
        compiler_params=pltpu.CompilerParams(vmem_limit_bytes=ALL_VMEM),
        name="prepare",
    )(pair, ln_gain.reshape(1, channels), w_bias.T)


def order_of_slots(z, along):
    near = [(z, 0), (z, along - 1), (z, 1), (1 - z, 0)]
    return near + [(z, along - 2), (1 - z, along - 1), (1 - z, 1), (1 - z, 2)]


def run_gate(arrays):
    return pl.pallas_call(
        gate,
        out_shape=jax.ShapeDtypeStruct((8, 128), f32),
        in_specs=[HBM] * len(arrays),
        out_specs=VMEM,
        compiler_params=pltpu.CompilerParams(vmem_limit_bytes=1 << 20),
        name="gate",
    )(*arrays)


def run_attend(length, own, other, parts, weights, passed, heads):
    blocks, each, width, channels = own.shape
    slots = len(parts)
    keys, queries = blocks * width, slots * width
    head = channels // heads
    return pl.pallas_call(
        functools.partial(attend, heads=heads, scale=head**-0.5, slots=slots),
        out_shape=jax.ShapeDtypeStruct((2, slots, each, width, channels), bf16),
        in_specs=[SMEM] + [HBM] * (slots + 8),
        out_specs=VMEM,
        scratch_shapes=[
            pltpu.VMEM((5, channels, channels), bf16),
            pltpu.SemaphoreType.DMA((5,)),
            pltpu.VMEM((slots, *parts[0].shape), bf16),
            pltpu.SemaphoreType.DMA((slots,)),
            pltpu.VMEM((2, *own.shape), bf16),
            pltpu.SemaphoreType.DMA((2,)),
            pltpu.VMEM((heads, keys, queries), f32),
        ]
        + [pltpu.VMEM((keys, channels), bf16)] * 2
        + [pltpu.VMEM((heads, head + 16, keys), bf16)] * 2
        + [pltpu.VMEM((heads, queries, channels), bf16)] * 2
        + [pltpu.VMEM((channels, queries), f32)] * 2
        + [pltpu.VMEM((channels, queries), bf16)] * 2
        + [pltpu.VMEM((keys, queries), f32)] * 2,
        compiler_params=pltpu.CompilerParams(vmem_limit_bytes=24 << 20),
        cost_estimate=pl.CostEstimate(flops=2_500_000_000, transcendentals=7_000_000, bytes_accessed=4_000_000),
        name="attend",
    )(length, own, other, *parts, *weights, passed)


def shifted(value, axis, by):
    n = lax.axis_size(axis)
    return lax.ppermute(value, axis, [(k, (k + by) % n) for k in range(n)])


def per_device_inner(pair, ln_gain, w_query, w_key, w_value, w_gate, w_bias, w_out, valid_length):
    tile_rows, tile_cols, channels = pair.shape
    heads = w_bias.shape[1]
    across = lax.axis_size(COL)
    each = tile_rows // across
    weights = [pltpu.with_memory_space_constraint(w, pltpu.HBM) for w in (w_query, w_key, w_value, w_gate, w_out)]
    normed, bias = run_prepare(pair, ln_gain, w_bias, across)
    mine = lax.all_to_all(bias, COL, 0, 0, tiled=True)
    own = lax.all_to_all(normed.reshape(across, each, tile_cols, channels), COL, 0, 0, tiled=True)
    below = shifted(mine, "z_lo", 1)
    left = shifted(mine, "x", 1)
    right = shifted(mine, "x", -1)
    below_left = shifted(below, "x", 1)
    below_right = shifted(below, "x", -1)
    far = shifted(left, "x", 1)
    below_far = shifted(below_right, "x", -1)
    passed = run_gate([right, below_left, far, below_far])
    other = shifted(own, "core", 1)
    parts = [mine, left, right, below, far, below_left, below_right, below_far]
    out = run_attend(valid_length, own, other, parts, weights, passed, heads)
    theirs = shifted(out[1], "core", 1)
    core = lax.axis_index("core")
    even = jnp.where(core == 0, out[0], theirs)
    odd = jnp.where(core == 0, theirs, out[0])
    update = jnp.stack([even, odd], axis=1).reshape(tile_rows, tile_cols, channels)
    return lax.all_to_all(update, COL, 0, 0, tiled=True)


def solution(mesh):
    fine = Mesh(mesh.devices.reshape(2, 4, 2, 4, 4), ROW + COL)
    placed = (P(ROW, COL, None), P(), P(), P(), P(), P(), P(), P(), P())
    return jax.shard_map(per_device_inner, mesh=fine, in_specs=placed, out_specs=P(ROW, COL, None), check_vma=False)
```

```python
import functools
import jax
import jax.numpy as jnp
from jax import lax
from jax.experimental import pallas as pl
from jax.experimental.pallas import tpu as pltpu
from jax.sharding import Mesh, PartitionSpec as P

epsilon = 1e-05
bf16, f32 = jnp.bfloat16, jnp.float32


def contract(a, b, da, db):
    return lax.dot_general(a, b, (((da,), (db,)), ((), ())), preferred_element_type=f32)


def prepare(pair_hbm, gain_hbm, w_hbm, normed_hbm, bias_out, *refs, step):
    pair_ref, sems, normed_ref, normed_sems, gain_ref, w_ref, small_sems, wide_ref = refs
    rows, cols, channels = pair_ref.shape
    heads = w_ref.shape[0]
    half = cols // 2
    lanes = wide_ref.shape[1]
    fetches = [
        pltpu.make_async_copy(pair_hbm.at[pl.ds(g * step, step)], pair_ref.at[pl.ds(g * step, step)], sems.at[g])
        for g in range(rows // step)
    ]
    small = [
        pltpu.make_async_copy(w_hbm, w_ref, small_sems.at[0]),
        pltpu.make_async_copy(gain_hbm, gain_ref, small_sems.at[1]),
    ]
    for fetch in fetches[:1] + small + fetches[1:]:
        fetch.start()
    for fetch in small:
        fetch.wait()
    gain = gain_ref[...]
    slots = 2 * heads
    mine = lax.axis_index("z_lo") * lax.axis_size("x") + lax.axis_index("x")

    def segment(count):
        slot = lax.broadcasted_iota(jnp.int32, (count, lanes), 1) // rows
        return lax.rem(slot + slots - mine, slots)

    own_head = lax.rem(segment(heads), heads) == lax.broadcasted_iota(jnp.int32, (heads, lanes), 0)
    wide_ref[...] = contract(w_ref[...], jnp.where(own_head, 1.0, 0.0).astype(bf16), 0, 0).astype(bf16)
    first = segment(half) < heads
    lane_j = lax.rem(lax.broadcasted_iota(jnp.int32, (half, lanes), 1), rows)
    acc = jnp.zeros((half, lanes), f32)
    stores = []
    for g, fetch in enumerate(fetches):
        fetch.wait()
        start = g * step
        x = pair_ref[pl.ds(start, step)].reshape(step * cols, channels).astype(f32)
        centred = x - jnp.mean(x, -1, keepdims=True)
        spread = jnp.mean(centred * centred, -1, keepdims=True)
        normed = (centred * lax.rsqrt(spread + epsilon) * gain).astype(bf16)
        normed_ref[pl.ds(start, step)] = normed.reshape(step, cols, channels)
        part = pl.ds(start, step)
        stores.append(pltpu.make_async_copy(normed_ref.at[part], normed_hbm.at[part], normed_sems.at[g]))
        stores[-1].start()
        wide = contract(normed, wide_ref[...], 1, 0)
        for t in range(step):
            one = wide[t * cols : (t + 1) * cols]
            both = jnp.where(first, one[:half], one[half:])
            acc = jnp.where(lane_j == start + t, both, acc)
    bias = acc.astype(bf16)
    for c in range(bias_out.shape[0]):
        bias_out[c] = bias
    for store in stores:
        store.wait()


def gate(*refs):
    refs[-1][...] = jnp.zeros_like(refs[-1])


def attend(length_ref, own_hbm, other_hbm, *refs, heads, scale, slots):
    parts_hbm, weights_hbm, refs = refs[:slots], refs[slots : slots + 5], refs[slots + 6 :]
    out_ref, weights, sems, parts, part_sems, both, both_sems = refs[:7]
    table = refs[7]
    keys_of, values_of, queries_of, gates_of, gated_of, scores_of = [refs[n : n + 2] for n in range(8, 20, 2)]
    _, blocks, each, width, channels = both.shape
    half = width // 2
    head = channels // heads
    keys, queries = blocks * width, slots * width
    core, x, z = lax.axis_index("core"), lax.axis_index("x"), lax.axis_index("z_lo")
    along = lax.axis_size("x")
    places = [zz * along + lax.rem(x + by, along) for zz, by in order_of_slots(z, along)]
    fetches = [pltpu.make_async_copy(p, parts.at[q], part_sems.at[n]) for n, (p, q) in enumerate(zip(parts_hbm, places))]
    later = [pltpu.make_async_copy(w, weights.at[n], sems.at[n]) for n, w in enumerate(weights_hbm)]
    later += [pltpu.make_async_copy(r, both.at[n], both_sems.at[n]) for n, r in enumerate((own_hbm, other_hbm))]
    for copy in fetches + later:
        copy.start()
    length = length_ref[0]
    base = (lax.axis_index("y") * lax.axis_size("z_hi") + lax.axis_index("z_hi")) * each
    own_base = (2 * (z * along + x) + core) * (each * blocks) + base
    other_base = (2 * (z * along + x) + 1 - core) * (each * blocks) + base
    for ref in values_of:
        ref[:, head:] = jnp.ones_like(ref[:, head:])
    for copy in fetches:
        copy.wait()
    place = lax.broadcasted_iota(jnp.int32, (half, 128), 1)

    def build(c, carry):
        pieces = [parts[q, c].astype(f32) for q in range(slots)]
        for kh in range(2):
            start = pl.multiple_of(c * width + kh * half, 8)
            valid = start + lax.broadcasted_iota(jnp.int32, (half, 128), 0) < length
            for h in range(heads):
                columns = []
                for at in range(0, queries, 128):
                    inside = range(at // width, -(-(at + 128) // width))
                    value = None
                    for p in inside:
                        new = pieces[(p - kh * heads - h) % slots][:, at : at + 128]
                        value = new if value is None else jnp.where(place >= p * width - at, new, value)
                    columns.append(value)
                if kh == 1:
                    turned = [pltpu.roll(v, 64, 1) for v in columns]
                    columns = [jnp.where(place < 64, turned[(n + 1) % 3], turned[(n + 2) % 3]) for n in range(3)]
                for n, value in enumerate(columns):
                    table[h, pl.ds(start, half), n * 128 : (n + 1) * 128] = jnp.where(valid, value, -1e30)
        return carry

    sizes = [keys * n // 6 for n in (4, 5, 6)]
    filled = jnp.int32(blocks)
    for used in reversed(sizes[:-1]):
        filled = jnp.where(length <= used, -(-used // width), filled)
    lax.fori_loop(0, filled, build, 0)
    for copy in later:
        copy.wait()
    wq, wk, wo = weights[0], weights[1], weights[4]
    wv = weights[2].T
    wg = weights[3].T
    lane = lax.broadcasted_iota(jnp.int32, (width, channels), 1)
    of_head = [(lane >= h * head) & (lane < (h + 1) * head) for h in range(heads)]

    def all_rows(used):
        def cells(n, chosen):
            side, t = n // each, lax.rem(n, each)
            return jnp.concatenate([both[side, c, t] for c in chosen], axis=0)

        def project_keys(n, to):
            keys_of[to][:used] = contract(cells(n, range(-(-used // width)))[:used], wk, 1, 0).astype(bf16)

        def project_values(n, to):
            value = contract(wv, cells(n, range(-(-used // width)))[:used], 1, 1).astype(bf16)
            for h in range(heads):
                values_of[to][h, :head, :used] = value[h * head : (h + 1) * head]

        def project_queries(n, to):
            asked = cells(n, [2 * q + core for q in range(slots)])
            query = (contract(asked, wq, 1, 0) * scale).astype(bf16)
            for h in range(heads):
                for p in range(slots):
                    q = (p - h) % slots
                    block = query[q * width : (q + 1) * width]
                    queries_of[to][h, p * width : (p + 1) * width] = jnp.where(of_head[h], block, jnp.zeros_like(block))

        def project_gates(n, to):
            asked = cells(n, [2 * q + core for q in range(slots)])
            gates_of[to][...] = jax.nn.sigmoid(contract(wg, asked, 1, 1)).astype(bf16).astype(f32)

        def score(at, h):
            scores = contract(keys_of[at][:used], queries_of[at][h], 1, 1) + table[h, :used]
            scores_of[h % 2][:used] = scores
            return jnp.max(scores.reshape(used // 8, 8, queries), 0)

        def blend(at, h, highest):
            exponent = jnp.exp(scores_of[h % 2][:used] - highest).astype(bf16)
            return contract(values_of[at][h, :, :used], exponent, 1, 0)

        def one_row(n, at, top):
            following = jnp.minimum(n + 1, 2 * each - 1)
            for h in range(heads):
                highest = jnp.max(top, 0, keepdims=True)
                top = score(at, h + 1) if h + 1 < heads else score(1 - at, 0)
                total = blend(at, h, highest)
                if h == 0:
                    project_keys(following, 1 - at)
                    project_queries(following, 1 - at)
                if h == 1:
                    project_values(following, 1 - at)
                if h == 2:
                    project_gates(following, 1 - at)
                blended = total[:head] / total[head : head + 1]
                if h > 0:
                    blended = jnp.concatenate([blended[:, h * width :], blended[:, : h * width]], axis=1)
                part = slice(h * head, (h + 1) * head)
                gated_of[at][part] = (gates_of[at][part] * blended).astype(bf16)
            update = contract(gated_of[at][...], wo, 0, 0)
            side, t = n // each, lax.rem(n, each)
            row_ok = jnp.where(side == 0, own_base, other_base) + t < length
            row = lax.broadcasted_iota(jnp.int32, (width, channels), 0)
            for q in range(slots):
                ok = (row + (2 * q + core) * width < length) & row_ok
                piece = update[q * width : (q + 1) * width]
                out_ref[side, q, t] = jnp.where(ok, piece, 0.0).astype(bf16)
            return top

        for first in (project_keys, project_queries, project_values, project_gates):
            first(0, 0)
        lax.fori_loop(0, each, lambda n, top: one_row(2 * n + 1, 1, one_row(2 * n, 0, top)), score(0, 0))

    for n, used in enumerate(sizes):
        fits = length <= used
        if n > 0:
            fits = fits & (length > sizes[n - 1])
        pl.when(fits)(functools.partial(all_rows, used))


ROW, COL = ("z_lo", "x", "core"), ("y", "z_hi")
VMEM = pl.BlockSpec(memory_space=pltpu.VMEM)
HBM = pl.BlockSpec(memory_space=pltpu.HBM)
SMEM = pl.BlockSpec(memory_space=pltpu.SMEM)


def in_hbm(value):
    return pltpu.with_memory_space_constraint(value, pltpu.HBM)


def run_prepare(pair, ln_gain, w_bias, across):
    tile_rows, tile_cols, channels = pair.shape
    heads = w_bias.shape[1]
    half = tile_cols // 2
    lanes = 2 * heads * tile_rows
    step = 12
    return pl.pallas_call(
        functools.partial(prepare, step=step),
        out_shape=(
            jax.ShapeDtypeStruct(pair.shape, bf16),
            jax.ShapeDtypeStruct((across, half, lanes), bf16),
        ),
        in_specs=[HBM] * 3,
        out_specs=(HBM, VMEM),
        scratch_shapes=[
            pltpu.VMEM(pair.shape, bf16),
            pltpu.SemaphoreType.DMA((tile_rows // step,)),
            pltpu.VMEM(pair.shape, bf16),
            pltpu.SemaphoreType.DMA((tile_rows // step,)),
            pltpu.VMEM((1, channels), f32),
            pltpu.VMEM((heads, channels), bf16),
            pltpu.SemaphoreType.DMA((2,)),
            pltpu.VMEM((channels, lanes), bf16),
        ],
        compiler_params=pltpu.CompilerParams(vmem_limit_bytes=16 << 20),
        name="prepare",
    )(*[in_hbm(v) for v in (pair, ln_gain.reshape(1, channels), w_bias.T)])


def order_of_slots(z, along):
    near = [(z, 0), (z, along - 1), (z, 1), (1 - z, 0)]
    return near + [(z, along - 2), (1 - z, along - 1), (1 - z, 1), (1 - z, 2)]


def run_gate(arrays):
    return pl.pallas_call(
        gate,
        out_shape=jax.ShapeDtypeStruct((8, 128), f32),
        in_specs=[HBM] * len(arrays),
        out_specs=VMEM,
        compiler_params=pltpu.CompilerParams(vmem_limit_bytes=1 << 20),
        name="gate",
    )(*arrays)


def run_attend(length, own, other, parts, weights, passed, heads):
    blocks, each, width, channels = own.shape
    slots = len(parts)
    keys, queries = blocks * width, slots * width
    head = channels // heads
    return pl.pallas_call(
        functools.partial(attend, heads=heads, scale=head**-0.5, slots=slots),
        out_shape=jax.ShapeDtypeStruct((2, slots, each, width, channels), bf16),
        in_specs=[SMEM] + [HBM] * (slots + 8),
        out_specs=VMEM,
        scratch_shapes=[
            pltpu.VMEM((5, channels, channels), bf16),
            pltpu.SemaphoreType.DMA((5,)),
            pltpu.VMEM((slots, *parts[0].shape), bf16),
            pltpu.SemaphoreType.DMA((slots,)),
            pltpu.VMEM((2, *own.shape), bf16),
            pltpu.SemaphoreType.DMA((2,)),
            pltpu.VMEM((heads, keys, queries), f32),
        ]
        + [pltpu.VMEM((keys, channels), bf16)] * 2
        + [pltpu.VMEM((heads, head + 16, keys), bf16)] * 2
        + [pltpu.VMEM((heads, queries, channels), bf16)] * 2
        + [pltpu.VMEM((channels, queries), f32)] * 2
        + [pltpu.VMEM((channels, queries), bf16)] * 2
        + [pltpu.VMEM((keys, queries), f32)] * 2,
        compiler_params=pltpu.CompilerParams(vmem_limit_bytes=24 << 20),
        cost_estimate=pl.CostEstimate(flops=2_500_000_000, transcendentals=7_000_000, bytes_accessed=4_000_000),
        name="attend",
    )(length, own, other, *parts, *weights, passed)


def shifted(value, axis, by):
    n = lax.axis_size(axis)
    return lax.ppermute(value, axis, [(k, (k + by) % n) for k in range(n)])


def per_device_inner(pair, ln_gain, w_query, w_key, w_value, w_gate, w_bias, w_out, valid_length):
    tile_rows, tile_cols, channels = pair.shape
    heads = w_bias.shape[1]
    across = lax.axis_size(COL)
    each = tile_rows // across
    weights = [in_hbm(w) for w in (w_query, w_key, w_value, w_gate, w_out)]
    normed, bias = run_prepare(pair, ln_gain, w_bias, across)
    mine = lax.all_to_all(bias, COL, 0, 0, tiled=True)
    own = lax.all_to_all(normed.reshape(across, each, tile_cols, channels), COL, 0, 0, tiled=True)
    below = shifted(mine, "z_lo", 1)
    left = shifted(mine, "x", 1)
    right = shifted(mine, "x", -1)
    below_left = shifted(below, "x", 1)
    below_right = shifted(below, "x", -1)
    far = shifted(left, "x", 1)
    below_far = shifted(below_right, "x", -1)
    passed = run_gate([right, below_left, far, below_far])
    other = shifted(own, "core", 1)
    parts = [mine, left, right, below, far, below_left, below_right, below_far]
    out = run_attend(valid_length, own, other, parts, weights, passed, heads)
    theirs = shifted(out[1], "core", 1)
    core = lax.axis_index("core")
    even = jnp.where(core == 0, out[0], theirs)
    odd = jnp.where(core == 0, theirs, out[0])
    update = jnp.stack([even, odd], axis=1).reshape(tile_rows, tile_cols, channels)
    return lax.all_to_all(update, COL, 0, 0, tiled=True)


def solution(mesh):
    fine = Mesh(mesh.devices.reshape(2, 4, 2, 4, 4), ROW + COL)
    placed = (P(ROW, COL, None), P(), P(), P(), P(), P(), P(), P(), P())
    return jax.shard_map(per_device_inner, mesh=fine, in_specs=placed, out_specs=P(ROW, COL, None), check_vma=False)
```

```python
import functools
import jax
import jax.numpy as jnp
from jax import lax
from jax.experimental import pallas as pl
from jax.experimental.pallas import tpu as pltpu
from jax.sharding import Mesh, PartitionSpec as P

epsilon = 1e-05
bf16, f32 = jnp.bfloat16, jnp.float32


def contract(a, b, da, db):
    return lax.dot_general(a, b, (((da,), (db,)), ((), ())), preferred_element_type=f32)


def prepare(pair_hbm, gain_hbm, w_hbm, normed_hbm, bias_out, *refs, cuts):
    pair_ref, sems, normed_ref, normed_sems, gain_ref, w_ref, small_sems, wide_ref = refs
    rows, cols, channels = pair_ref.shape
    heads = w_ref.shape[0]
    half = cols // 2
    lanes = wide_ref.shape[1]
    runs = [pl.ds(start, stop - start) for start, stop in zip(cuts, cuts[1:])]
    fetches = [pltpu.make_async_copy(pair_hbm.at[r], pair_ref.at[r], sems.at[g]) for g, r in enumerate(runs)]
    small = [
        pltpu.make_async_copy(w_hbm, w_ref, small_sems.at[0]),
        pltpu.make_async_copy(gain_hbm, gain_ref, small_sems.at[1]),
    ]
    for fetch in fetches[:1] + small + fetches[1:]:
        fetch.start()
    for fetch in small:
        fetch.wait()
    gain = gain_ref[...]
    slots = 2 * heads
    mine = lax.axis_index("z_lo") * lax.axis_size("x") + lax.axis_index("x")

    def segment(count):
        slot = lax.broadcasted_iota(jnp.int32, (count, lanes), 1) // rows
        return lax.rem(slot + slots - mine, slots)

    own_head = lax.rem(segment(heads), heads) == lax.broadcasted_iota(jnp.int32, (heads, lanes), 0)
    wide_ref[...] = contract(w_ref[...], jnp.where(own_head, 1.0, 0.0).astype(bf16), 0, 0).astype(bf16)
    first = segment(half) < heads
    lane_j = lax.rem(lax.broadcasted_iota(jnp.int32, (half, lanes), 1), rows)
    acc = jnp.zeros((half, lanes), f32)
    stores = []
    for g, fetch in enumerate(fetches):
        fetch.wait()
        start, step = cuts[g], cuts[g + 1] - cuts[g]
        x = pair_ref[pl.ds(start, step)].reshape(step * cols, channels).astype(f32)
        centred = x - jnp.mean(x, -1, keepdims=True)
        spread = jnp.mean(centred * centred, -1, keepdims=True)
        normed = (centred * lax.rsqrt(spread + epsilon) * gain).astype(bf16)
        normed_ref[pl.ds(start, step)] = normed.reshape(step, cols, channels)
        part = pl.ds(start, step)
        stores.append(pltpu.make_async_copy(normed_ref.at[part], normed_hbm.at[part], normed_sems.at[g]))
        stores[-1].start()
        wide = contract(normed, wide_ref[...], 1, 0)
        for t in range(step):
            one = wide[t * cols : (t + 1) * cols]
            both = jnp.where(first, one[:half], one[half:])
            acc = jnp.where(lane_j == start + t, both, acc)
    bias = acc.astype(bf16)
    for c in range(bias_out.shape[0]):
        bias_out[c] = bias
    for store in stores:
        store.wait()


def gate(*refs):
    refs[-1][...] = jnp.zeros_like(refs[-1])


def key_sizes(keys):
    return [keys * n // 6 for n in (4, 5, 6)]


def build_table(length_ref, *refs, heads, width):
    slots = len(refs) - 3
    parts_in, (table, parts, part_sems) = refs[:slots], refs[slots:]
    _, blocks, half, queries = parts.shape
    keys = blocks * width
    x, z = lax.axis_index("x"), lax.axis_index("z_lo")
    along = lax.axis_size("x")
    places = [zz * along + lax.rem(x + by, along) for zz, by in order_of_slots(z, along)]
    fetches = [pltpu.make_async_copy(p, parts.at[q], part_sems.at[n]) for n, (p, q) in enumerate(zip(parts_in, places))]
    for fetch in fetches:
        fetch.start()
    length = length_ref[0]
    for fetch in fetches:
        fetch.wait()
    place = lax.broadcasted_iota(jnp.int32, (half, 128), 1)

    def build(c, carry):
        pieces = [parts[q, c].astype(f32) for q in range(slots)]
        for kh in range(2):
            start = pl.multiple_of(c * width + kh * half, 8)
            valid = start + lax.broadcasted_iota(jnp.int32, (half, 128), 0) < length
            for h in range(heads):
                columns = []
                for at in range(0, queries, 128):
                    inside = range(at // width, -(-(at + 128) // width))
                    value = None
                    for p in inside:
                        new = pieces[(p - kh * heads - h) % slots][:, at : at + 128]
                        value = new if value is None else jnp.where(place >= p * width - at, new, value)
                    columns.append(value)
                if kh == 1:
                    turned = [pltpu.roll(v, 64, 1) for v in columns]
                    columns = [jnp.where(place < 64, turned[(n + 1) % 3], turned[(n + 2) % 3]) for n in range(3)]
                for n, value in enumerate(columns):
                    table[h, pl.ds(start, half), n * 128 : (n + 1) * 128] = jnp.where(valid, value, -1e30)
        return carry

    sizes = key_sizes(keys)
    filled = jnp.int32(blocks)
    for used in reversed(sizes[:-1]):
        filled = jnp.where(length <= used, -(-used // width), filled)
    lax.fori_loop(0, filled, build, 0)


def attend(length_ref, own_ref, other_ref, table, *refs, heads, scale, slots):
    weights_hbm, refs = refs[:5], refs[6:]
    out_ref, weights, sems = refs[:3]
    keys_of, values_of, queries_of, gates_of, gated_of, scores_of = [refs[n : n + 2] for n in range(3, 15, 2)]
    later = [pltpu.make_async_copy(w, weights.at[n], sems.at[n]) for n, w in enumerate(weights_hbm)]
    for copy in later:
        copy.start()
    sides = (own_ref, other_ref)
    blocks, each, width, channels = own_ref.shape
    head = channels // heads
    keys, queries = blocks * width, slots * width
    core, x, z = lax.axis_index("core"), lax.axis_index("x"), lax.axis_index("z_lo")
    along = lax.axis_size("x")
    length = length_ref[0]
    base = (lax.axis_index("y") * lax.axis_size("z_hi") + lax.axis_index("z_hi")) * each
    bases = [(2 * (z * along + x) + near) * (each * blocks) + base for near in (core, 1 - core)]
    for ref in values_of:
        ref[:, head:] = jnp.ones_like(ref[:, head:])
    for ref in gated_of:
        ref[...] = jnp.zeros_like(ref)
    for copy in later:
        copy.wait()
    wq, wk, wo = weights[0], weights[1], weights[4]
    wv = weights[2].T
    wg = weights[3].T
    lane = lax.broadcasted_iota(jnp.int32, (width, channels), 1)
    of_head = [(lane >= h * head) & (lane < (h + 1) * head) for h in range(heads)]

    def all_rows(used):
        def cells(t, side, chosen):
            return jnp.concatenate([sides[side][c, t] for c in chosen], axis=0)

        def project_keys(t, to):
            keys_of[to][:used] = contract(cells(t, to, range(-(-used // width)))[:used], wk, 1, 0).astype(bf16)

        def project_values(t, to):
            value = contract(wv, cells(t, to, range(-(-used // width)))[:used], 1, 1).astype(bf16)
            for h in range(heads):
                values_of[to][h, :head, :used] = value[h * head : (h + 1) * head]

        def project_queries(t, to):
            asked = cells(t, to, [2 * q + core for q in range(slots)])
            query = (contract(asked, wq, 1, 0) * scale).astype(bf16)
            for h in range(heads):
                for p in range(slots):
                    q = (p - h) % slots
                    block = query[q * width : (q + 1) * width]
                    queries_of[to][h, p * width : (p + 1) * width] = jnp.where(of_head[h], block, jnp.zeros_like(block))

        def project_gates(t, to):
            asked = cells(t, to, [2 * q + core for q in range(slots)])
            gates_of[to][...] = jax.nn.sigmoid(contract(wg, asked, 1, 1)).astype(bf16).astype(f32)

        def score(at, h):
            scores = contract(keys_of[at][:used], queries_of[at][h], 1, 1) + table[h, :used]
            scores_of[h % 2][:used] = scores
            return jnp.max(scores.reshape(used // 8, 8, queries), 0)

        def blend(at, h, highest):
            exponent = jnp.exp(scores_of[h % 2][:used] - highest).astype(bf16)
            return contract(values_of[at][h, :, :used], exponent, 1, 0)

        def finish(t, at):
            update = contract(gated_of[at][...], wo, 0, 0)
            row_ok = bases[at] + t < length
            row = lax.broadcasted_iota(jnp.int32, (width, channels), 0)
            for q in range(slots):
                ok = (row + (2 * q + core) * width < length) & row_ok
                piece = update[q * width : (q + 1) * width]
                out_ref[at, q, t] = jnp.where(ok, piece, 0.0).astype(bf16)

        def one_row(at, before, following, top):
            for h in range(heads):
                highest = jnp.max(top, 0, keepdims=True)
                top = score(at, h + 1) if h + 1 < heads else score(1 - at, 0)
                total = blend(at, h, highest)
                if h == 0:
                    project_keys(following, 1 - at)
                    project_queries(following, 1 - at)
                if h == 1:
                    project_values(following, 1 - at)
                if h == 2:
                    project_gates(following, 1 - at)
                    finish(before, 1 - at)
                blended = total[:head] / total[head : head + 1]
                if h > 0:
                    blended = jnp.concatenate([blended[:, h * width :], blended[:, : h * width]], axis=1)
                part = slice(h * head, (h + 1) * head)
                gated_of[at][part] = (gates_of[at][part] * blended).astype(bf16)
            return top

        def two_rows(t, top):
            top = one_row(0, jnp.maximum(t - 1, 0), t, top)
            return one_row(1, t, jnp.minimum(t + 1, each - 1), top)

        for first in (project_keys, project_queries, project_values, project_gates):
            first(0, 0)
        lax.fori_loop(0, each, two_rows, score(0, 0))
        finish(each - 1, 1)

    sizes = key_sizes(keys)
    for n, used in enumerate(sizes):
        fits = length <= used
        if n > 0:
            fits = fits & (length > sizes[n - 1])
        pl.when(fits)(functools.partial(all_rows, used))


ROW, COL = ("z_lo", "x", "core"), ("y", "z_hi")
VMEM = pl.BlockSpec(memory_space=pltpu.VMEM)
HBM = pl.BlockSpec(memory_space=pltpu.HBM)
SMEM = pl.BlockSpec(memory_space=pltpu.SMEM)


def in_hbm(value):
    return pltpu.with_memory_space_constraint(value, pltpu.HBM)


def run_prepare(pair, ln_gain, w_bias, across):
    tile_rows, tile_cols, channels = pair.shape
    heads = w_bias.shape[1]
    half = tile_cols // 2
    lanes = 2 * heads * tile_rows
    cuts = [tile_rows * n // 6 for n in (0, 1, 3, 5, 6)]
    return pl.pallas_call(
        functools.partial(prepare, cuts=cuts),
        out_shape=(
            jax.ShapeDtypeStruct(pair.shape, bf16),
            jax.ShapeDtypeStruct((across, half, lanes), bf16),
        ),
        in_specs=[HBM] * 3,
        out_specs=(HBM, VMEM),
        scratch_shapes=[
            pltpu.VMEM(pair.shape, bf16),
            pltpu.SemaphoreType.DMA((len(cuts) - 1,)),
            pltpu.VMEM(pair.shape, bf16),
            pltpu.SemaphoreType.DMA((len(cuts) - 1,)),
            pltpu.VMEM((1, channels), f32),
            pltpu.VMEM((heads, channels), bf16),
            pltpu.SemaphoreType.DMA((2,)),
            pltpu.VMEM((channels, lanes), bf16),
        ],
        compiler_params=pltpu.CompilerParams(vmem_limit_bytes=16 << 20),
        name="prepare",
    )(*[in_hbm(v) for v in (pair, ln_gain.reshape(1, channels), w_bias.T)])


def order_of_slots(z, along):
    near = [(z, 0), (z, along - 1), (z, 1), (1 - z, 0)]
    return near + [(z, along - 2), (1 - z, along - 1), (1 - z, 1), (1 - z, 2)]


def run_gate(arrays):
    return pl.pallas_call(
        gate,
        out_shape=jax.ShapeDtypeStruct((8, 128), f32),
        in_specs=[HBM] * len(arrays),
        out_specs=VMEM,
        compiler_params=pltpu.CompilerParams(vmem_limit_bytes=1 << 20),
        name="gate",
    )(*arrays)


def run_build(length, parts, heads, width):
    slots = len(parts)
    blocks, half, lanes = parts[0].shape
    return pl.pallas_call(
        functools.partial(build_table, heads=heads, width=width),
        out_shape=jax.ShapeDtypeStruct((heads, blocks * width, slots * width), f32),
        in_specs=[SMEM] + [HBM] * slots,
        out_specs=VMEM,
        scratch_shapes=[pltpu.VMEM((slots, blocks, half, lanes), bf16), pltpu.SemaphoreType.DMA((slots,))],
        compiler_params=pltpu.CompilerParams(vmem_limit_bytes=8 << 20),
        cost_estimate=pl.CostEstimate(flops=4_000_000, transcendentals=0, bytes_accessed=7_000_000),
        name="build",
    )(length, *parts)


def run_attend(length, own, other, table, weights, passed):
    _, each, width, channels = own.shape
    heads, keys, queries = table.shape
    slots = queries // width
    head = channels // heads
    return pl.pallas_call(
        functools.partial(attend, heads=heads, scale=head**-0.5, slots=slots),
        out_shape=jax.ShapeDtypeStruct((2, slots, each, width, channels), bf16),
        in_specs=[SMEM] + [VMEM] * 3 + [HBM] * 6,
        out_specs=VMEM,
        scratch_shapes=[
            pltpu.VMEM((5, channels, channels), bf16),
            pltpu.SemaphoreType.DMA((5,)),
        ]
        + [pltpu.VMEM((keys, channels), bf16)] * 2
        + [pltpu.VMEM((heads, head + 16, keys), bf16)] * 2
        + [pltpu.VMEM((heads, queries, channels), bf16)] * 2
        + [pltpu.VMEM((channels, queries), f32)] * 2
        + [pltpu.VMEM((channels, queries), bf16)] * 2
        + [pltpu.VMEM((keys, queries), f32)] * 2,
        compiler_params=pltpu.CompilerParams(vmem_limit_bytes=20 << 20),
        cost_estimate=pl.CostEstimate(flops=2_500_000_000, transcendentals=7_000_000, bytes_accessed=4_000_000),
        name="attend",
    )(length, own, other, table, *weights, passed)


def shifted(value, axis, by):
    n = lax.axis_size(axis)
    return lax.ppermute(value, axis, [(k, (k + by) % n) for k in range(n)])


def per_device_inner(pair, ln_gain, w_query, w_key, w_value, w_gate, w_bias, w_out, valid_length):
    tile_rows, tile_cols, channels = pair.shape
    heads = w_bias.shape[1]
    across = lax.axis_size(COL)
    each = tile_rows // across
    weights = [in_hbm(w) for w in (w_query, w_key, w_value, w_gate, w_out)]
    normed, bias = run_prepare(pair, ln_gain, w_bias, across)
    mine = lax.all_to_all(bias, COL, 0, 0, tiled=True)
    own = lax.all_to_all(normed.reshape(across, each, tile_cols, channels), COL, 0, 0, tiled=True)
    below = shifted(mine, "z_lo", 1)
    left = shifted(mine, "x", 1)
    right = shifted(mine, "x", -1)
    below_left = shifted(below, "x", 1)
    below_right = shifted(below, "x", -1)
    far = shifted(left, "x", 1)
    below_far = shifted(below_right, "x", -1)
    passed = run_gate([right, below_left, far, below_far])
    other = shifted(own, "core", 1)
    parts = [mine, left, right, below, far, below_left, below_right, below_far]
    table = run_build(valid_length, parts, heads, tile_cols)
    out = run_attend(valid_length, own, other, table, weights, passed)
    theirs = shifted(out[1], "core", 1)
    core = lax.axis_index("core")
    even = jnp.where(core == 0, out[0], theirs)
    odd = jnp.where(core == 0, theirs, out[0])
    update = jnp.stack([even, odd], axis=1).reshape(tile_rows, tile_cols, channels)
    return lax.all_to_all(update, COL, 0, 0, tiled=True)


def solution(mesh):
    fine = Mesh(mesh.devices.reshape(2, 4, 2, 4, 4), ROW + COL)
    placed = (P(ROW, COL, None), P(), P(), P(), P(), P(), P(), P(), P())
    return jax.shard_map(per_device_inner, mesh=fine, in_specs=placed, out_specs=P(ROW, COL, None), check_vma=False)
```

```python
import functools
import jax
import jax.numpy as jnp
from jax import lax
from jax.experimental import pallas as pl
from jax.experimental.pallas import tpu as pltpu
from jax.sharding import Mesh, PartitionSpec as P

epsilon = 1e-05
bf16, f32 = jnp.bfloat16, jnp.float32


def contract(a, b, da, db):
    return lax.dot_general(a, b, (((da,), (db,)), ((), ())), preferred_element_type=f32)


def prepare(pair_hbm, gain_hbm, w_hbm, normed_hbm, bias_out, *refs, cuts):
    pair_ref, sems, normed_ref, normed_sems, gain_ref, w_ref, small_sems, wide_ref = refs
    rows, cols, channels = pair_ref.shape
    heads = w_ref.shape[0]
    half = cols // 2
    lanes = wide_ref.shape[1]
    runs = [pl.ds(start, stop - start) for start, stop in zip(cuts, cuts[1:])]
    fetches = [pltpu.make_async_copy(pair_hbm.at[r], pair_ref.at[r], sems.at[g]) for g, r in enumerate(runs)]
    small = [
        pltpu.make_async_copy(w_hbm, w_ref, small_sems.at[0]),
        pltpu.make_async_copy(gain_hbm, gain_ref, small_sems.at[1]),
    ]
    for fetch in fetches[:1] + small + fetches[1:]:
        fetch.start()
    for fetch in small:
        fetch.wait()
    gain = gain_ref[...]
    slots = 2 * heads
    mine = lax.axis_index("z_lo") * lax.axis_size("x") + lax.axis_index("x")

    def segment(count):
        slot = lax.broadcasted_iota(jnp.int32, (count, lanes), 1) // rows
        return lax.rem(slot + slots - mine, slots)

    own_head = lax.rem(segment(heads), heads) == lax.broadcasted_iota(jnp.int32, (heads, lanes), 0)
    wide_ref[...] = contract(w_ref[...], jnp.where(own_head, 1.0, 0.0).astype(bf16), 0, 0).astype(bf16)
    first = segment(half) < heads
    lane_j = lax.rem(lax.broadcasted_iota(jnp.int32, (half, lanes), 1), rows)
    acc = jnp.zeros((half, lanes), f32)
    stores = []
    for g, fetch in enumerate(fetches):
        fetch.wait()
        start, step = cuts[g], cuts[g + 1] - cuts[g]
        x = pair_ref[pl.ds(start, step)].reshape(step * cols, channels).astype(f32)
        centred = x - jnp.mean(x, -1, keepdims=True)
        spread = jnp.mean(centred * centred, -1, keepdims=True)
        normed = (centred * lax.rsqrt(spread + epsilon) * gain).astype(bf16)
        normed_ref[pl.ds(start, step)] = normed.reshape(step, cols, channels)
        part = pl.ds(start, step)
        stores.append(pltpu.make_async_copy(normed_ref.at[part], normed_hbm.at[part], normed_sems.at[g]))
        stores[-1].start()
        wide = contract(normed, wide_ref[...], 1, 0)
        for t in range(step):
            one = wide[t * cols : (t + 1) * cols]
            both = jnp.where(first, one[:half], one[half:])
            acc = jnp.where(lane_j == start + t, both, acc)
    bias = acc.astype(bf16)
    for c in range(bias_out.shape[0]):
        bias_out[c] = bias
    for store in stores:
        store.wait()


def deliver(source, target, sems):
    count = sems.shape[0]
    step = source.shape[0] // count
    copies = []
    for n in range(count):
        part = pl.ds(n * step, step)
        copies.append(pltpu.make_async_copy(source.at[part], target.at[part], sems.at[n]))
        copies[-1].start()
    for copy in copies:
        copy.wait()


def gate(*refs):
    refs[-1][...] = jnp.zeros_like(refs[-1])


def key_sizes(keys):
    return [keys * n // 12 for n in (8, 9, 10, 11, 12)]


def build_table(length_ref, *refs, heads, width):
    slots = len(refs) - 10
    parts_in, weights_hbm, (table, weights, parts, part_sems, sems) = refs[:slots], refs[slots : slots + 5], refs[slots + 5 :]
    _, blocks, half, queries = parts.shape
    keys = blocks * width
    x, z = lax.axis_index("x"), lax.axis_index("z_lo")
    along = lax.axis_size("x")
    places = [zz * along + lax.rem(x + by, along) for zz, by in order_of_slots(z, along)]
    fetches = [pltpu.make_async_copy(p, parts.at[q], part_sems.at[n]) for n, (p, q) in enumerate(zip(parts_in, places))]
    copies = [pltpu.make_async_copy(w, weights.at[n], sems.at[n]) for n, w in enumerate(weights_hbm)]
    for fetch in copies + fetches:
        fetch.start()
    length = length_ref[0]
    for fetch in fetches:
        fetch.wait()
    place = lax.broadcasted_iota(jnp.int32, (half, 128), 1)

    def build(c, carry):
        pieces = [parts[q, c].astype(f32) for q in range(slots)]
        for kh in range(2):
            start = pl.multiple_of(c * width + kh * half, 8)
            valid = start + lax.broadcasted_iota(jnp.int32, (half, 128), 0) < length
            for h in range(heads):
                columns = []
                for at in range(0, queries, 128):
                    inside = range(at // width, -(-(at + 128) // width))
                    value = None
                    for p in inside:
                        new = pieces[(p - kh * heads - h) % slots][:, at : at + 128]
                        value = new if value is None else jnp.where(place >= p * width - at, new, value)
                    columns.append(value)
                if kh == 1:
                    turned = [pltpu.roll(v, 64, 1) for v in columns]
                    columns = [jnp.where(place < 64, turned[(n + 1) % 3], turned[(n + 2) % 3]) for n in range(3)]
                for n, value in enumerate(columns):
                    table[h, pl.ds(start, half), n * 128 : (n + 1) * 128] = jnp.where(valid, value, -1e30)
        return carry

    sizes = key_sizes(keys)
    filled = jnp.int32(blocks)
    for used in reversed(sizes[:-1]):
        filled = jnp.where(length <= used, -(-used // width), filled)
    lax.fori_loop(0, filled, build, 0)
    for copy in copies:
        copy.wait()


def attend(length_ref, own_ref, other_ref, table, weights, passed, out_ref, *refs, heads, scale, slots):
    keys_of, values_of, queries_of, gates_of, gated_of, scores_of = [refs[n : n + 2] for n in range(0, 12, 2)]
    sides = (own_ref, other_ref)
    blocks, each, width, channels = own_ref.shape
    head = channels // heads
    keys, queries = blocks * width, slots * width
    core, x, z = lax.axis_index("core"), lax.axis_index("x"), lax.axis_index("z_lo")
    along = lax.axis_size("x")
    length = length_ref[0]
    base = (lax.axis_index("y") * lax.axis_size("z_hi") + lax.axis_index("z_hi")) * each
    bases = [(2 * (z * along + x) + near) * (each * blocks) + base for near in (core, 1 - core)]
    for ref in values_of:
        ref[:, head:] = jnp.ones_like(ref[:, head:])
    for ref in gated_of:
        ref[...] = jnp.zeros_like(ref)
    wq, wk, wo = weights[0], weights[1], weights[4]
    wv = weights[2].T
    wg = weights[3].T
    lane = lax.broadcasted_iota(jnp.int32, (width, channels), 1)
    of_head = [(lane >= h * head) & (lane < (h + 1) * head) for h in range(heads)]

    def all_rows(used):
        def cells(t, side, chosen):
            return jnp.concatenate([sides[side][c, t] for c in chosen], axis=0)

        def project_keys(t, to):
            keys_of[to][:used] = contract(cells(t, to, range(-(-used // width)))[:used], wk, 1, 0).astype(bf16)

        def project_values(t, to):
            value = contract(wv, cells(t, to, range(-(-used // width)))[:used], 1, 1).astype(bf16)
            for h in range(heads):
                values_of[to][h, :head, :used] = value[h * head : (h + 1) * head]

        def project_queries(t, to):
            asked = cells(t, to, [2 * q + core for q in range(slots)])
            query = (contract(asked, wq, 1, 0) * scale).astype(bf16)
            for h in range(heads):
                for p in range(slots):
                    q = (p - h) % slots
                    block = query[q * width : (q + 1) * width]
                    queries_of[to][h, p * width : (p + 1) * width] = jnp.where(of_head[h], block, jnp.zeros_like(block))

        def project_gates(t, to):
            asked = cells(t, to, [2 * q + core for q in range(slots)])
            gates_of[to][...] = jax.nn.sigmoid(contract(wg, asked, 1, 1)).astype(bf16).astype(f32)

        def score(at, h):
            scores = contract(keys_of[at][:used], queries_of[at][h], 1, 1) + table[h, :used]
            scores_of[h % 2][:used] = scores
            return jnp.max(scores.reshape(used // 8, 8, queries), 0)

        def blend(at, h, highest):
            exponent = jnp.exp(scores_of[h % 2][:used] - highest).astype(bf16)
            return contract(values_of[at][h, :, :used], exponent, 1, 0)

        def finish(t, at):
            update = contract(gated_of[at][...], wo, 0, 0)
            row_ok = bases[at] + t < length
            row = lax.broadcasted_iota(jnp.int32, (width, channels), 0)
            for q in range(slots):
                ok = (row + (2 * q + core) * width < length) & row_ok
                piece = update[q * width : (q + 1) * width]
                out_ref[at, q, t] = jnp.where(ok, piece, 0.0).astype(bf16)

        def one_row(at, before, following, top):
            for h in range(heads):
                highest = jnp.max(top, 0, keepdims=True)
                top = score(at, h + 1) if h + 1 < heads else score(1 - at, 0)
                total = blend(at, h, highest)
                if h == 0:
                    project_keys(following, 1 - at)
                    project_queries(following, 1 - at)
                if h == 1:
                    project_values(following, 1 - at)
                if h == 2:
                    project_gates(following, 1 - at)
                    finish(before, 1 - at)
                blended = total[:head] / total[head : head + 1]
                if h > 0:
                    blended = jnp.concatenate([blended[:, h * width :], blended[:, : h * width]], axis=1)
                part = slice(h * head, (h + 1) * head)
                gated_of[at][part] = (gates_of[at][part] * blended).astype(bf16)
            return top

        def two_rows(t, top):
            top = one_row(0, jnp.maximum(t - 1, 0), t, top)
            return one_row(1, t, jnp.minimum(t + 1, each - 1), top)

        for first in (project_keys, project_queries, project_values, project_gates):
            first(0, 0)
        lax.fori_loop(0, each, two_rows, score(0, 0))
        finish(each - 1, 1)

    sizes = key_sizes(keys)
    for n, used in enumerate(sizes):
        fits = length <= used
        if n > 0:
            fits = fits & (length > sizes[n - 1])
        pl.when(fits)(functools.partial(all_rows, used))


ROW, COL = ("z_lo", "x", "core"), ("y", "z_hi")
VMEM = pl.BlockSpec(memory_space=pltpu.VMEM)
HBM = pl.BlockSpec(memory_space=pltpu.HBM)
SMEM = pl.BlockSpec(memory_space=pltpu.SMEM)


def in_hbm(value):
    return pltpu.with_memory_space_constraint(value, pltpu.HBM)


def run_prepare(pair, ln_gain, w_bias, across):
    tile_rows, tile_cols, channels = pair.shape
    heads = w_bias.shape[1]
    half = tile_cols // 2
    lanes = 2 * heads * tile_rows
    cuts = [tile_rows * n // 6 for n in (0, 1, 6)]
    return pl.pallas_call(
        functools.partial(prepare, cuts=cuts),
        out_shape=(
            jax.ShapeDtypeStruct(pair.shape, bf16),
            jax.ShapeDtypeStruct((across, half, lanes), bf16),
        ),
        in_specs=[HBM] * 3,
        out_specs=(HBM, VMEM),
        scratch_shapes=[
            pltpu.VMEM(pair.shape, bf16),
            pltpu.SemaphoreType.DMA((len(cuts) - 1,)),
            pltpu.VMEM(pair.shape, bf16),
            pltpu.SemaphoreType.DMA((len(cuts) - 1,)),
            pltpu.VMEM((1, channels), f32),
            pltpu.VMEM((heads, channels), bf16),
            pltpu.SemaphoreType.DMA((2,)),
            pltpu.VMEM((channels, lanes), bf16),
        ],
        compiler_params=pltpu.CompilerParams(vmem_limit_bytes=16 << 20),
        name="prepare",
    )(*[in_hbm(v) for v in (pair, ln_gain.reshape(1, channels), w_bias.T)])


def order_of_slots(z, along):
    near = [(z, 0), (z, along - 1), (z, 1), (1 - z, 0)]
    return near + [(z, along - 2), (1 - z, along - 1), (1 - z, 1), (1 - z, 2)]


def run_gate(arrays):
    return pl.pallas_call(
        gate,
        out_shape=jax.ShapeDtypeStruct((8, 128), f32),
        in_specs=[HBM] * len(arrays),
        out_specs=VMEM,
        compiler_params=pltpu.CompilerParams(vmem_limit_bytes=1 << 20),
        name="gate",
    )(*arrays)


def run_build(length, parts, weights, heads, width):
    slots = len(parts)
    blocks, half, lanes = parts[0].shape
    packed = (len(weights), *weights[0].shape)
    return pl.pallas_call(
        functools.partial(build_table, heads=heads, width=width),
        out_shape=(
            jax.ShapeDtypeStruct((heads, blocks * width, slots * width), f32),
            jax.ShapeDtypeStruct(packed, bf16),
        ),
        in_specs=[SMEM] + [HBM] * (slots + len(weights)),
        out_specs=(VMEM, VMEM),
        scratch_shapes=[
            pltpu.VMEM((slots, blocks, half, lanes), bf16),
            pltpu.SemaphoreType.DMA((slots,)),
            pltpu.SemaphoreType.DMA((len(weights),)),
        ],
        compiler_params=pltpu.CompilerParams(vmem_limit_bytes=8 << 20),
        cost_estimate=pl.CostEstimate(flops=4_000_000, transcendentals=0, bytes_accessed=7_000_000),
        name="build",
    )(length, *parts, *weights)


def run_attend(length, own, other, table, weights, passed):
    _, each, width, channels = own.shape
    heads, keys, queries = table.shape
    slots = queries // width
    head = channels // heads
    return pl.pallas_call(
        functools.partial(attend, heads=heads, scale=head**-0.5, slots=slots),
        out_shape=jax.ShapeDtypeStruct((2, slots, each, width, channels), bf16),
        in_specs=[SMEM] + [VMEM] * 4 + [HBM],
        out_specs=VMEM,
        scratch_shapes=[pltpu.VMEM((keys, channels), bf16)] * 2
        + [pltpu.VMEM((heads, head + 16, keys), bf16)] * 2
        + [pltpu.VMEM((heads, queries, channels), bf16)] * 2
        + [pltpu.VMEM((channels, queries), f32)] * 2
        + [pltpu.VMEM((channels, queries), bf16)] * 2
        + [pltpu.VMEM((keys, queries), f32)] * 2,
        compiler_params=pltpu.CompilerParams(vmem_limit_bytes=20 << 20),
        cost_estimate=pl.CostEstimate(flops=2_500_000_000, transcendentals=7_000_000, bytes_accessed=4_000_000),
        name="attend",
    )(length, own, other, table, weights, passed)


def run_deliver(value):
    return pl.pallas_call(
        deliver,
        out_shape=jax.ShapeDtypeStruct(value.shape, value.dtype),
        in_specs=[VMEM],
        out_specs=HBM,
        scratch_shapes=[pltpu.SemaphoreType.DMA((6,))],
        compiler_params=pltpu.CompilerParams(vmem_limit_bytes=1 << 20),
        name="deliver",
    )(value)


def shifted(value, axis, by):
    n = lax.axis_size(axis)
    return lax.ppermute(value, axis, [(k, (k + by) % n) for k in range(n)])


def per_device_inner(pair, ln_gain, w_query, w_key, w_value, w_gate, w_bias, w_out, valid_length):
    tile_rows, tile_cols, channels = pair.shape
    heads = w_bias.shape[1]
    across = lax.axis_size(COL)
    each = tile_rows // across
    weights = [in_hbm(w) for w in (w_query, w_key, w_value, w_gate, w_out)]
    normed, bias = run_prepare(pair, ln_gain, w_bias, across)
    mine = lax.all_to_all(bias, COL, 0, 0, tiled=True)
    own = lax.all_to_all(normed.reshape(across, each, tile_cols, channels), COL, 0, 0, tiled=True)
    below = shifted(mine, "z_lo", 1)
    left = shifted(mine, "x", 1)
    right = shifted(mine, "x", -1)
    below_left = shifted(below, "x", 1)
    below_right = shifted(below, "x", -1)
    far = shifted(left, "x", 1)
    below_far = shifted(below_right, "x", -1)
    passed = run_gate([right, below_left, far, below_far])
    other = shifted(own, "core", 1)
    parts = [mine, left, right, below, far, below_left, below_right, below_far]
    table, weights = run_build(valid_length, parts, weights, heads, tile_cols)
    out = run_attend(valid_length, own, other, table, weights, passed)
    theirs = shifted(out[1], "core", 1)
    core = lax.axis_index("core")
    even = jnp.where(core == 0, out[0], theirs)
    odd = jnp.where(core == 0, theirs, out[0])
    update = jnp.stack([even, odd], axis=1).reshape(tile_rows, tile_cols, channels)
    return run_deliver(lax.all_to_all(update, COL, 0, 0, tiled=True))


def solution(mesh):
    fine = Mesh(mesh.devices.reshape(2, 4, 2, 4, 4), ROW + COL)
    placed = (P(ROW, COL, None), P(), P(), P(), P(), P(), P(), P(), P())
    return jax.shard_map(per_device_inner, mesh=fine, in_specs=placed, out_specs=P(ROW, COL, None), check_vma=False)
```

```python
import functools
import jax
import jax.numpy as jnp
from jax import lax
from jax.experimental import pallas as pl
from jax.experimental.pallas import tpu as pltpu
from jax.sharding import Mesh, PartitionSpec as P

epsilon = 1e-05
bf16, f32 = jnp.bfloat16, jnp.float32


def contract(a, b, da, db):
    return lax.dot_general(a, b, (((da,), (db,)), ((), ())), preferred_element_type=f32)


def prepare(pair_hbm, gain_hbm, w_hbm, normed_hbm, bias_out, *refs, cuts):
    pair_ref, sems, normed_ref, normed_sems, gain_ref, w_ref, small_sems, wide_ref = refs
    rows, cols, channels = pair_ref.shape
    heads = w_ref.shape[0]
    half = cols // 2
    lanes = wide_ref.shape[1]
    runs = [pl.ds(start, stop - start) for start, stop in zip(cuts, cuts[1:])]
    fetches = [pltpu.make_async_copy(pair_hbm.at[r], pair_ref.at[r], sems.at[g]) for g, r in enumerate(runs)]
    small = [
        pltpu.make_async_copy(w_hbm, w_ref, small_sems.at[0]),
        pltpu.make_async_copy(gain_hbm, gain_ref, small_sems.at[1]),
    ]
    for fetch in fetches[:1] + small + fetches[1:]:
        fetch.start()
    for fetch in small:
        fetch.wait()
    gain = gain_ref[...]
    slots = 2 * heads
    mine = lax.axis_index("z_lo") * lax.axis_size("x") + lax.axis_index("x")

    def segment(count):
        slot = lax.broadcasted_iota(jnp.int32, (count, lanes), 1) // rows
        return lax.rem(slot + slots - mine, slots)

    own_head = lax.rem(segment(heads), heads) == lax.broadcasted_iota(jnp.int32, (heads, lanes), 0)
    wide_ref[...] = contract(w_ref[...], jnp.where(own_head, 1.0, 0.0).astype(bf16), 0, 0).astype(bf16)
    first = segment(half) < heads
    lane_j = lax.rem(lax.broadcasted_iota(jnp.int32, (half, lanes), 1), rows)
    acc = jnp.zeros((half, lanes), f32)
    stores = []
    for g, fetch in enumerate(fetches):
        fetch.wait()
        start, step = cuts[g], cuts[g + 1] - cuts[g]
        x = pair_ref[pl.ds(start, step)].reshape(step * cols, channels).astype(f32)
        centred = x - jnp.mean(x, -1, keepdims=True)
        spread = jnp.mean(centred * centred, -1, keepdims=True)
        normed = (centred * lax.rsqrt(spread + epsilon) * gain).astype(bf16)
        normed_ref[pl.ds(start, step)] = normed.reshape(step, cols, channels)
        part = pl.ds(start, step)
        stores.append(pltpu.make_async_copy(normed_ref.at[part], normed_hbm.at[part], normed_sems.at[g]))
        stores[-1].start()
        wide = contract(normed, wide_ref[...], 1, 0)
        for t in range(step):
            one = wide[t * cols : (t + 1) * cols]
            both = jnp.where(first, one[:half], one[half:])
            acc = jnp.where(lane_j == start + t, both, acc)
    bias = acc.astype(bf16)
    for c in range(bias_out.shape[0]):
        bias_out[c] = bias
    for store in stores:
        store.wait()


def gate(*refs):
    refs[-1][...] = jnp.zeros_like(refs[-1])


def key_sizes(keys):
    return [keys * n // 12 for n in (8, 9, 10, 11, 12)]


def build_table(length_ref, *refs, heads, width):
    slots = len(refs) - 10
    parts_in, weights_hbm, (table, weights, parts, part_sems, sems) = refs[:slots], refs[slots : slots + 5], refs[slots + 5 :]
    _, blocks, half, queries = parts.shape
    keys = blocks * width
    x, z = lax.axis_index("x"), lax.axis_index("z_lo")
    along = lax.axis_size("x")
    places = [zz * along + lax.rem(x + by, along) for zz, by in order_of_slots(z, along)]
    fetches = [pltpu.make_async_copy(p, parts.at[q], part_sems.at[n]) for n, (p, q) in enumerate(zip(parts_in, places))]
    copies = [pltpu.make_async_copy(w, weights.at[n], sems.at[n]) for n, w in enumerate(weights_hbm)]
    for fetch in copies + fetches:
        fetch.start()
    length = length_ref[0]
    for fetch in fetches:
        fetch.wait()
    place = lax.broadcasted_iota(jnp.int32, (half, 128), 1)

    def build(c, carry):
        pieces = [parts[q, c].astype(f32) for q in range(slots)]
        for kh in range(2):
            start = pl.multiple_of(c * width + kh * half, 8)
            valid = start + lax.broadcasted_iota(jnp.int32, (half, 128), 0) < length
            for h in range(heads):
                columns = []
                for at in range(0, queries, 128):
                    inside = range(at // width, -(-(at + 128) // width))
                    value = None
                    for p in inside:
                        new = pieces[(p - kh * heads - h) % slots][:, at : at + 128]
                        value = new if value is None else jnp.where(place >= p * width - at, new, value)
                    columns.append(value)
                if kh == 1:
                    turned = [pltpu.roll(v, 64, 1) for v in columns]
                    columns = [jnp.where(place < 64, turned[(n + 1) % 3], turned[(n + 2) % 3]) for n in range(3)]
                for n, value in enumerate(columns):
                    table[h, pl.ds(start, half), n * 128 : (n + 1) * 128] = jnp.where(valid, value, -1e30)
        return carry

    sizes = key_sizes(keys)
    filled = jnp.int32(blocks)
    for used in reversed(sizes[:-1]):
        filled = jnp.where(length <= used, -(-used // width), filled)
    lax.fori_loop(0, filled, build, 0)
    for copy in copies:
        copy.wait()


def attend(length_ref, own_ref, other_ref, table, weights, passed, out_ref, *refs, heads, scale, slots):
    keys_of, values_of, queries_of, gates_of, gated_of, scores_of = [refs[n : n + 2] for n in range(0, 12, 2)]
    sides = (own_ref, other_ref)
    blocks, each, width, channels = own_ref.shape
    head = channels // heads
    keys, queries = blocks * width, slots * width
    core, x, z = lax.axis_index("core"), lax.axis_index("x"), lax.axis_index("z_lo")
    along = lax.axis_size("x")
    length = length_ref[0]
    base = (lax.axis_index("y") * lax.axis_size("z_hi") + lax.axis_index("z_hi")) * each
    bases = [(2 * (z * along + x) + near) * (each * blocks) + base for near in (core, 1 - core)]
    for ref in values_of:
        ref[:, head:] = jnp.ones_like(ref[:, head:])
    for ref in gated_of:
        ref[...] = jnp.zeros_like(ref)
    wq, wk, wo = weights[0], weights[1], weights[4]
    wv = weights[2].T
    wg = weights[3].T
    lane = lax.broadcasted_iota(jnp.int32, (width, channels), 1)
    of_head = [(lane >= h * head) & (lane < (h + 1) * head) for h in range(heads)]

    def all_rows(used):
        def cells(t, side, chosen):
            return jnp.concatenate([sides[side][c, t] for c in chosen], axis=0)

        def project_keys(t, to):
            keys_of[to][:used] = contract(cells(t, to, range(-(-used // width)))[:used], wk, 1, 0).astype(bf16)

        def project_values(t, to):
            value = contract(wv, cells(t, to, range(-(-used // width)))[:used], 1, 1).astype(bf16)
            for h in range(heads):
                values_of[to][h, :head, :used] = value[h * head : (h + 1) * head]

        def project_queries(t, to):
            asked = cells(t, to, [2 * q + core for q in range(slots)])
            query = (contract(asked, wq, 1, 0) * scale).astype(bf16)
            for h in range(heads):
                for p in range(slots):
                    q = (p - h) % slots
                    block = query[q * width : (q + 1) * width]
                    queries_of[to][h, p * width : (p + 1) * width] = jnp.where(of_head[h], block, jnp.zeros_like(block))

        def project_gates(t, to):
            asked = cells(t, to, [2 * q + core for q in range(slots)])
            gates_of[to][...] = jax.nn.sigmoid(contract(wg, asked, 1, 1)).astype(bf16).astype(f32)

        def score(at, h):
            scores = contract(keys_of[at][:used], queries_of[at][h], 1, 1) + table[h, :used]
            scores_of[h % 2][:used] = scores
            return jnp.max(scores.reshape(used // 8, 8, queries), 0)

        def blend(at, h, highest):
            exponent = jnp.exp(scores_of[h % 2][:used] - highest).astype(bf16)
            return contract(values_of[at][h, :, :used], exponent, 1, 0)

        def finish(t, at):
            update = contract(gated_of[at][...], wo, 0, 0)
            row_ok = bases[at] + t < length
            row = lax.broadcasted_iota(jnp.int32, (width, channels), 0)
            for q in range(slots):
                ok = (row + (2 * q + core) * width < length) & row_ok
                piece = update[q * width : (q + 1) * width]
                out_ref[at, q, t] = jnp.where(ok, piece, 0.0).astype(bf16)

        def one_row(at, before, following, top):
            for h in range(heads):
                highest = jnp.max(top, 0, keepdims=True)
                top = score(at, h + 1) if h + 1 < heads else score(1 - at, 0)
                total = blend(at, h, highest)
                if h == 0:
                    project_keys(following, 1 - at)
                    project_queries(following, 1 - at)
                if h == 1:
                    project_values(following, 1 - at)
                if h == 2:
                    project_gates(following, 1 - at)
                    finish(before, 1 - at)
                blended = total[:head] / total[head : head + 1]
                if h > 0:
                    blended = jnp.concatenate([blended[:, h * width :], blended[:, : h * width]], axis=1)
                part = slice(h * head, (h + 1) * head)
                gated_of[at][part] = (gates_of[at][part] * blended).astype(bf16)
            return top

        def two_rows(t, top):
            top = one_row(0, jnp.maximum(t - 1, 0), t, top)
            return one_row(1, t, jnp.minimum(t + 1, each - 1), top)

        for first in (project_keys, project_queries, project_values, project_gates):
            first(0, 0)
        lax.fori_loop(0, each, two_rows, score(0, 0))
        finish(each - 1, 1)

    sizes = key_sizes(keys)
    for n, used in enumerate(sizes):
        fits = length <= used
        if n > 0:
            fits = fits & (length > sizes[n - 1])
        pl.when(fits)(functools.partial(all_rows, used))


ROW, COL = ("z_lo", "x", "core"), ("y", "z_hi")
VMEM = pl.BlockSpec(memory_space=pltpu.VMEM)
HBM = pl.BlockSpec(memory_space=pltpu.HBM)
SMEM = pl.BlockSpec(memory_space=pltpu.SMEM)


def in_hbm(value):
    return pltpu.with_memory_space_constraint(value, pltpu.HBM)


def run_prepare(pair, ln_gain, w_bias, across):
    tile_rows, tile_cols, channels = pair.shape
    heads = w_bias.shape[1]
    half = tile_cols // 2
    lanes = 2 * heads * tile_rows
    cuts = [tile_rows * n // 6 for n in (0, 1, 6)]
    return pl.pallas_call(
        functools.partial(prepare, cuts=cuts),
        out_shape=(
            jax.ShapeDtypeStruct(pair.shape, bf16),
            jax.ShapeDtypeStruct((across, half, lanes), bf16),
        ),
        in_specs=[HBM] * 3,
        out_specs=(HBM, VMEM),
        scratch_shapes=[
            pltpu.VMEM(pair.shape, bf16),
            pltpu.SemaphoreType.DMA((len(cuts) - 1,)),
            pltpu.VMEM(pair.shape, bf16),
            pltpu.SemaphoreType.DMA((len(cuts) - 1,)),
            pltpu.VMEM((1, channels), f32),
            pltpu.VMEM((heads, channels), bf16),
            pltpu.SemaphoreType.DMA((2,)),
            pltpu.VMEM((channels, lanes), bf16),
        ],
        compiler_params=pltpu.CompilerParams(vmem_limit_bytes=16 << 20),
        name="prepare",
    )(*[in_hbm(v) for v in (pair, ln_gain.reshape(1, channels), w_bias.T)])


def order_of_slots(z, along):
    near = [(z, 0), (z, along - 1), (z, 1), (1 - z, 0)]
    return near + [(z, along - 2), (1 - z, along - 1), (1 - z, 1), (1 - z, 2)]


def run_gate(arrays):
    return pl.pallas_call(
        gate,
        out_shape=jax.ShapeDtypeStruct((8, 128), f32),
        in_specs=[HBM] * len(arrays),
        out_specs=VMEM,
        compiler_params=pltpu.CompilerParams(vmem_limit_bytes=1 << 20),
        name="gate",
    )(*arrays)


def run_build(length, parts, weights, heads, width):
    slots = len(parts)
    blocks, half, lanes = parts[0].shape
    packed = (len(weights), *weights[0].shape)
    return pl.pallas_call(
        functools.partial(build_table, heads=heads, width=width),
        out_shape=(
            jax.ShapeDtypeStruct((heads, blocks * width, slots * width), f32),
            jax.ShapeDtypeStruct(packed, bf16),
        ),
        in_specs=[SMEM] + [HBM] * (slots + len(weights)),
        out_specs=(VMEM, VMEM),
        scratch_shapes=[
            pltpu.VMEM((slots, blocks, half, lanes), bf16),
            pltpu.SemaphoreType.DMA((slots,)),
            pltpu.SemaphoreType.DMA((len(weights),)),
        ],
        compiler_params=pltpu.CompilerParams(vmem_limit_bytes=8 << 20),
        cost_estimate=pl.CostEstimate(flops=4_000_000, transcendentals=0, bytes_accessed=7_000_000),
        name="build",
    )(length, *parts, *weights)


def run_attend(length, own, other, table, weights, passed):
    _, each, width, channels = own.shape
    heads, keys, queries = table.shape
    slots = queries // width
    head = channels // heads
    return pl.pallas_call(
        functools.partial(attend, heads=heads, scale=head**-0.5, slots=slots),
        out_shape=jax.ShapeDtypeStruct((2, slots, each, width, channels), bf16),
        in_specs=[SMEM] + [VMEM] * 4 + [HBM],
        out_specs=VMEM,
        scratch_shapes=[pltpu.VMEM((keys, channels), bf16)] * 2
        + [pltpu.VMEM((heads, head + 16, keys), bf16)] * 2
        + [pltpu.VMEM((heads, queries, channels), bf16)] * 2
        + [pltpu.VMEM((channels, queries), f32)] * 2
        + [pltpu.VMEM((channels, queries), bf16)] * 2
        + [pltpu.VMEM((keys, queries), f32)] * 2,
        compiler_params=pltpu.CompilerParams(vmem_limit_bytes=20 << 20),
        cost_estimate=pl.CostEstimate(flops=2_500_000_000, transcendentals=7_000_000, bytes_accessed=4_000_000),
        name="attend",
    )(length, own, other, table, weights, passed)


def shifted(value, axis, by):
    n = lax.axis_size(axis)
    return lax.ppermute(value, axis, [(k, (k + by) % n) for k in range(n)])


def per_device_inner(pair, ln_gain, w_query, w_key, w_value, w_gate, w_bias, w_out, valid_length):
    tile_rows, tile_cols, channels = pair.shape
    heads = w_bias.shape[1]
    across = lax.axis_size(COL)
    each = tile_rows // across
    weights = [in_hbm(w) for w in (w_query, w_key, w_value, w_gate, w_out)]
    normed, bias = run_prepare(pair, ln_gain, w_bias, across)
    mine = lax.all_to_all(bias, COL, 0, 0, tiled=True)
    own = lax.all_to_all(normed.reshape(across, each, tile_cols, channels), COL, 0, 0, tiled=True)
    below = shifted(mine, "z_lo", 1)
    left = shifted(mine, "x", 1)
    right = shifted(mine, "x", -1)
    below_left = shifted(below, "x", 1)
    below_right = shifted(below, "x", -1)
    far = shifted(left, "x", 1)
    below_far = shifted(below_right, "x", -1)
    passed = run_gate([right, below_left, far, below_far])
    other = shifted(own, "core", 1)
    parts = [mine, left, right, below, far, below_left, below_right, below_far]
    table, weights = run_build(valid_length, parts, weights, heads, tile_cols)
    out = run_attend(valid_length, own, other, table, weights, passed)
    theirs = shifted(out[1], "core", 1)
    core = lax.axis_index("core")
    even = jnp.where(core == 0, out[0], theirs)
    odd = jnp.where(core == 0, theirs, out[0])
    update = jnp.stack([even, odd], axis=1).reshape(tile_rows, tile_cols, channels)
    return lax.all_to_all(update, COL, 0, 0, tiled=True)


def solution(mesh):
    fine = Mesh(mesh.devices.reshape(2, 4, 2, 4, 4), ROW + COL)
    placed = (P(ROW, COL, None), P(), P(), P(), P(), P(), P(), P(), P())
    return jax.shard_map(per_device_inner, mesh=fine, in_specs=placed, out_specs=P(ROW, COL, None), check_vma=False)
```
